128 devices in a mesh: slab: 8 (over y, core), seq: 16 (over z, x).
Axes of the slice: x: 4, y: 4, z: 4, core: 2. Of those that a mesh axis runs over, the one named last changes fastest.
Arguments:
- query: bfloat16 [32768, 3072], P(('slab', 'seq')), may hold values from -9 to 9
- key: bfloat16 [32768, 3072], P(('slab', 'seq')), may hold values from -9 to 9
- value: bfloat16 [32768, 3072], P(('slab', 'seq')), may hold values from -6 to 6
- d_out: bfloat16 [32768, 3072], P(('slab', 'seq')), may hold values from -6 to 6
- pattern: int32 [48, 256, 8], P('seq', 'slab'), may hold values from 0 to 255, as said below
Outputs:
- attended: bfloat16 [32768, 3072], P(('slab', 'seq'))
- grad_query: bfloat16 [32768, 3072], P(('slab', 'seq'))
- grad_key: bfloat16 [32768, 3072], P(('slab', 'seq'))
- grad_value: bfloat16 [32768, 3072], P(('slab', 'seq'))
The draws below stay inside these ranges and needn't reach their ends.
Inputs may be any that keep to these rules, and one draw needn't show every extreme that they name: Every list pattern[h, b] holds 8 distinct blocks: first b itself, then blocks of b's own slab, and blocks of the adjacent slabs only (slab of block k is k // 32). A list of a slab with two neighbours holds 2 blocks of each; a list of the first or the last slab holds 2 blocks of its one neighbour. For each slab and each adjacent slab, the lists of every head together reference exactly 4 blocks of that adjacent slab, the same set for all heads.
All inputs are finite; a program needn't handle non-finite values.
Results may differ from the reference program's by a relative error of at most 0.0081.
Values may be sent and summed in bfloat16 or wider, within the bound.
A program may use at most 128 MiB of HBM per device.

```python
import jax
import jax.numpy as jnp
from jax import lax

HEADS = 48
HDIM = 64
BLOCK = 128
KSEL = 8
CROSS = 4
D = 3072
SLAB_BLOCKS = 32
QBLOCKS = 256
TOKENS = 32768
N_SLAB = 8


def draw_query(key, part):
    values = jnp.clip(jax.random.normal(jax.random.fold_in(key, 1), (TOKENS, HEADS * HDIM), jnp.float32), -6.0, 6.0)
    return values.astype(jnp.bfloat16)


def draw_key(key, part):
    values = jnp.clip(jax.random.normal(jax.random.fold_in(key, 3), (TOKENS, HEADS * HDIM), jnp.float32), -6.0, 6.0)
    return values.astype(jnp.bfloat16)


def cross_sets(key):
    scores = jax.random.randint(key, (N_SLAB, SLAB_BLOCKS), 0, 65536, jnp.int32) * SLAB_BLOCKS
    scores = scores + jnp.arange(SLAB_BLOCKS, dtype=jnp.int32)[None, :]
    return lax.top_k(scores, CROSS)[1].astype(jnp.int32)


def neighbour_picks(key, salt, slab_ids, inside, shift_slab):
    sets = cross_sets(jax.random.fold_in(key, salt))
    offsets = jax.random.randint(jax.random.fold_in(key, salt + 10), (HEADS, N_SLAB), 0, CROSS, jnp.int32)
    half = CROSS // 2
    step_ids = jnp.arange(half, dtype=jnp.int32)
    positions = (offsets[:, slab_ids][:, :, None] + inside[None, :, None] + step_ids[None, None, :]) % CROSS
    per_block = jnp.broadcast_to(sets[slab_ids][None, :, :], (HEADS, QBLOCKS, CROSS))
    picked = jnp.take_along_axis(per_block, positions, axis=-1)
    return picked + ((slab_ids + shift_slab) * SLAB_BLOCKS)[None, :, None]


def draw_pattern(key, part):
    half = CROSS // 2
    locals_count = KSEL - 1 - CROSS
    block_ids = jnp.arange(QBLOCKS, dtype=jnp.int32)
    slab_ids = block_ids // SLAB_BLOCKS
    inside = block_ids % SLAB_BLOCKS
    below = neighbour_picks(key, 21, slab_ids, inside, -1)
    above = neighbour_picks(key, 22, slab_ids, inside, 1)
    nearby = jnp.arange(SLAB_BLOCKS, dtype=jnp.int32)
    scores = jax.random.randint(jax.random.fold_in(key, 24), (HEADS, QBLOCKS, SLAB_BLOCKS), 0, 65536, jnp.int32) * SLAB_BLOCKS
    scores = scores + nearby[None, None, :]
    scores = jnp.where((nearby[None, :] == inside[:, None])[None, :, :], -1, scores)
    own_picks = lax.top_k(scores, locals_count + half)[1].astype(jnp.int32) + (slab_ids * SLAB_BLOCKS)[None, :, None]
    first = own_picks[:, :, :locals_count]
    extra = own_picks[:, :, locals_count:]
    low_part = jnp.where((slab_ids == 0)[None, :, None], extra, below)
    high_part = jnp.where((slab_ids == N_SLAB - 1)[None, :, None], extra, above)
    own_block = jnp.broadcast_to(block_ids[None, :, None], (HEADS, QBLOCKS, 1))
    return jnp.concatenate([own_block, first, low_part, high_part], axis=-1).astype(jnp.int32)


def block_levels(stream_key, dims, shards, smallest, top_value):
    def one(dim, parts):
        steps = jax.random.uniform(jax.random.fold_in(jax.random.fold_in(stream_key, 6), dim), (parts,), jnp.float32, smallest / len(shards), top_value / len(shards))
        return jnp.repeat(jnp.exp(steps), dims[dim] // parts).reshape((-1,) + (1,) * (len(dims) - dim - 1))

    loudness = one(*shards[0])
    for cut in shards[1:]:
        loudness = loudness * one(*cut)
    return loudness


def scatter_about(stream_key, extent, width, limit, split=(), kind=jnp.bfloat16):
    result = jax.random.normal(stream_key, extent, jnp.float32) * width
    if len(split) > 0:
        result = block_levels(stream_key, extent, split, -0.22, 0.18) * result
    return jnp.clip(result, min=-limit, max=limit).astype(kind)


def setup_inputs(seed: int = 0) -> dict:
    keys = jax.random.split(jax.random.key(seed), 6)
    return {
        "query": draw_query(jax.random.fold_in(keys[5], 71), 0),
        "key": draw_key(jax.random.fold_in(keys[5], 71), 0),
        "value": scatter_about(keys[2], (TOKENS, D), 1.0, 6.0, ((0, 128),)),
        "d_out": scatter_about(keys[3], (TOKENS, D), 1.0, 6.0, ((0, 128),)),
        "pattern": draw_pattern(jax.random.fold_in(keys[5], 71), 0),
    }


def rounded(values):
    return lax.optimization_barrier(values.astype(jnp.bfloat16)).astype(jnp.float32)


def spread(contrib, lists, keep):
    masked = jnp.where(keep[:, :, None, None], contrib, jnp.zeros_like(contrib))
    flat_rows = masked.reshape(QBLOCKS * KSEL, BLOCK, HDIM)
    empty = jnp.zeros((QBLOCKS, BLOCK, HDIM), jnp.float32)
    return empty.at[lists.reshape(-1)].add(flat_rows)


def one_head(inputs):
    query_h, key_h, value_h, grad_h, lists = inputs
    scaling = HDIM ** -0.5
    query_f = query_h.astype(jnp.float32)
    key_f = key_h.astype(jnp.float32)
    value_f = value_h.astype(jnp.float32)
    grad_f = grad_h.astype(jnp.float32)
    key_sel = key_f[lists].reshape(QBLOCKS, KSEL * BLOCK, HDIM)
    value_sel = value_f[lists].reshape(QBLOCKS, KSEL * BLOCK, HDIM)
    scores = jnp.einsum("qid,qjd->qij", query_f, key_sel) * scaling
    row_max = jnp.max(scores, axis=-1, keepdims=True)
    weights = jnp.exp(scores - row_max)
    weights = weights / jnp.sum(weights, axis=-1, keepdims=True)
    weights_low = rounded(weights)
    attended = jnp.einsum("qij,qjd->qid", weights_low, value_sel).astype(jnp.bfloat16)
    grad_prob = jnp.einsum("qid,qjd->qij", grad_f, value_sel)
    correction = jnp.sum(weights * grad_prob, axis=-1, keepdims=True)
    grad_score = rounded(weights * (grad_prob - correction))
    grad_query = (jnp.einsum("qij,qjd->qid", grad_score, key_sel) * scaling).astype(jnp.bfloat16)
    key_terms = (jnp.einsum("qij,qid->qjd", grad_score, query_f) * scaling).reshape(QBLOCKS, KSEL, BLOCK, HDIM)
    value_terms = jnp.einsum("qij,qid->qjd", weights_low, grad_f).reshape(QBLOCKS, KSEL, BLOCK, HDIM)
    offset_slab = lists // SLAB_BLOCKS - (jnp.arange(QBLOCKS, dtype=jnp.int32) // SLAB_BLOCKS)[:, None]

    def combine(contrib):
        same_sum = spread(contrib, lists, offset_slab == 0)
        later_sum = spread(contrib, lists, offset_slab == -1)
        earlier_sum = spread(contrib, lists, offset_slab == 1)
        return (same_sum + rounded(later_sum) + rounded(earlier_sum)).astype(jnp.bfloat16)

    return attended, grad_query, combine(key_terms), combine(value_terms)


def heads_first(array):
    return array.reshape(QBLOCKS, BLOCK, HEADS, HDIM).transpose(2, 0, 1, 3)


def tokens_back(array):
    return array.transpose(1, 2, 0, 3).reshape(TOKENS, HEADS * HDIM)


def reference(query, key, value, d_out, pattern):
    results = lax.map(one_head, (heads_first(query), heads_first(key), heads_first(value), heads_first(d_out), pattern))
    return (tokens_back(results[0]), tokens_back(results[1]), tokens_back(results[2]), tokens_back(results[3]))
```

```python
import functools

import jax
import jax.numpy as jnp
from jax import lax
from jax.experimental import pallas as pl
from jax.experimental.pallas import tpu as pltpu
from jax.sharding import PartitionSpec as P

CROSS = 4
HDIM = 64
BLOCK = 128
SCALE = HDIM**-0.5


def from_behind(x, axis, by):
    count = lax.axis_size(axis)
    pairs = [(i, i + by) for i in range(count) if 0 <= i + by < count]
    return lax.ppermute(x, axis, pairs)


def pack_kernel(q_ref, k_ref, v_ref, g_ref, kv_ref, qg_ref):
    for t in range(3):
        cols = slice(128 * t, 128 * t + 128)
        q, k, v, g = q_ref[:, cols], k_ref[:, cols], v_ref[:, cols], g_ref[:, cols]
        q = q * jnp.asarray(SCALE, q.dtype)
        for i in range(2):
            head = 2 * t + i
            half = slice(64 * i, 64 * i + 64)
            kv_ref[head // 3, head % 3] = jnp.concatenate([k[:, half], v[:, half]], axis=1)
            qg_ref[head // 3, head % 3] = jnp.concatenate([q[:, half], g[:, half]], axis=1)


def pack(q, k, v, g):
    rows, columns = q.shape
    spec = pl.BlockSpec((rows, 384), lambda i: (0, i))
    out = jax.ShapeDtypeStruct((16, 3, rows, 128), q.dtype)
    out_spec = pl.BlockSpec((2, 3, rows, 128), lambda i: (i, 0, 0, 0))
    return pl.pallas_call(
        pack_kernel,
        grid=(8,),
        in_specs=[spec] * 4,
        out_specs=[out_spec] * 2,
        out_shape=[out] * 2,
        cost_estimate=pl.CostEstimate(flops=0, bytes_accessed=12 << 20, transcendentals=0),
        name="pack",
    )(q, k, v, g)


def unpack_kernel(og_ref, kv_ref, o_ref, dq_ref, dk_ref, dv_ref):
    for t in range(3):
        cols = slice(128 * t, 128 * t + 128)
        a, b = 2 * t, 2 * t + 1
        og_a, og_b = og_ref[a // 3, a % 3], og_ref[b // 3, b % 3]
        kv_a, kv_b = kv_ref[a // 3, a % 3], kv_ref[b // 3, b % 3]
        dq_ref[:, cols] = jnp.concatenate([og_a[:, :64], og_b[:, :64]], axis=1)
        o_ref[:, cols] = jnp.concatenate([og_a[:, 64:], og_b[:, 64:]], axis=1)
        dk_ref[:, cols] = jnp.concatenate([kv_a[:, :64], kv_b[:, :64]], axis=1)
        dv_ref[:, cols] = jnp.concatenate([kv_a[:, 64:], kv_b[:, 64:]], axis=1)


def unpack(og, kv):
    rows = og.shape[2]
    spec = pl.BlockSpec((2, 3, rows, 128), lambda i: (i, 0, 0, 0))
    out_spec = pl.BlockSpec((rows, 384), lambda i: (0, i))
    out = jax.ShapeDtypeStruct((rows, 3072), og.dtype)
    return pl.pallas_call(
        unpack_kernel,
        grid=(8,),
        in_specs=[spec] * 2,
        out_specs=[out_spec] * 4,
        out_shape=[out] * 4,
        cost_estimate=pl.CostEstimate(flops=0, bytes_accessed=12 << 20, transcendentals=0),
        name="unpack",
    )(og, kv)


def nt(a, b):
    return lax.dot_general(a, b, (((1,), (1,)), ((), ())), preferred_element_type=jnp.float32)


def attend_kernel(
    ids_ref, kv_ref, qg_ref, prev_ref, next_ref, og_ref, dkv_ref, cross_ref, kvw, kvt, acc, sd, ex, *, blocks, per_list
):
    head = pl.program_id(0)
    bf16 = jnp.bfloat16
    own = blocks

    @pl.loop(0, own // 2)
    def _(i):
        for half in range(2):
            block = kv_ref[i, 0, half * BLOCK : half * BLOCK + BLOCK]
            kvw[2 * i + half] = block
            kvt[2 * i + half] = block.T

    for c in range(CROSS):
        kvw[own + c] = prev_ref[0, c]
        kvt[own + c] = prev_ref[0, c].T
        kvw[own + CROSS + c] = next_ref[0, c]
        kvt[own + CROSS + c] = next_ref[0, c].T
    acc[...] = jnp.zeros_like(acc)
    left = lax.broadcasted_iota(jnp.int32, (BLOCK, 128), 1) < HDIM

    @pl.loop(0, blocks)
    def _(b):
        row = pl.multiple_of((b % 2) * BLOCK, BLOCK)
        qg = qg_ref[b // 2, 0, pl.ds(row, BLOCK)]
        zero = jnp.zeros_like(qg)
        both = jnp.concatenate([jnp.where(left, qg, zero), jnp.where(left, zero, qg)], axis=0)
        base = (head * blocks + b) * per_list
        ids = [ids_ref[base + j] for j in range(per_list)]
        top = None
        for j in range(per_list):
            pair = nt(kvw[ids[j]], both)
            sd[j] = pair
            part = jnp.max(pair[:, :BLOCK].reshape(16, 8, BLOCK), axis=0)
            top = part if top is None else jnp.maximum(top, part)
        row_max = jnp.max(top, axis=0, keepdims=True)
        total = jnp.zeros((8, BLOCK), jnp.float32)
        mixed = jnp.zeros((8, BLOCK), jnp.float32)
        for j in range(per_list):
            e = jnp.exp(sd[j, :, :BLOCK] - row_max)
            sd[j, :, :BLOCK] = e
            ex[j, :, BLOCK:] = e.astype(bf16)
            total += jnp.sum(e.reshape(16, 8, BLOCK), axis=0)
            mixed += jnp.sum((e * sd[j, :, BLOCK:]).reshape(16, 8, BLOCK), axis=0)
        inverse = 1.0 / jnp.sum(total, axis=0, keepdims=True)
        correction = jnp.sum(mixed, axis=0, keepdims=True) * inverse
        for j in range(per_list):
            ex[j, :, :BLOCK] = (sd[j, :, :BLOCK] * (sd[j, :, BLOCK:] - correction)).astype(bf16)
        out = jnp.zeros((128, 2 * BLOCK), jnp.float32)
        for j in range(0, per_list, 2):
            lhs = jnp.concatenate([kvt[ids[j]], kvt[ids[j + 1]]], axis=1)
            rhs = ex[j : j + 2].reshape(2 * BLOCK, 2 * BLOCK)
            out += jnp.dot(lhs, rhs, preferred_element_type=jnp.float32)
        outs = jnp.concatenate([out[:HDIM, :BLOCK] * (inverse * SCALE), out[HDIM:, BLOCK:] * inverse], axis=0)
        og_ref[b // 2, 0, pl.ds(row, BLOCK)] = outs.T.astype(bf16)
        column = jnp.broadcast_to(inverse, (BLOCK, BLOCK)).T
        scaled = (both.astype(jnp.float32) * jnp.concatenate([column, column], axis=0)).astype(bf16)
        for j in range(per_list):
            acc[ids[j]] += jnp.dot(ex[j], scaled, preferred_element_type=jnp.float32)

    @pl.loop(0, own // 2)
    def _(i):
        for half in range(2):
            dkv_ref[i, 0, half * BLOCK : half * BLOCK + BLOCK] = acc[2 * i + half].astype(bf16)

    for c in range(2 * CROSS):
        cross_ref[0, c] = acc[own + c].astype(bf16)


def attend(ids, kv, qg, prev, nxt):
    heads, blocks, per_list = ids.shape
    rows = kv.shape[2]
    whole = pl.BlockSpec((16, 1, rows, 128), lambda h, *_: (0, h, 0, 0))
    side = pl.BlockSpec((1, CROSS, BLOCK, 128), lambda h, *_: (h, 0, 0, 0))
    window = blocks + 2 * CROSS
    f32, bf16 = jnp.float32, jnp.bfloat16
    return pl.pallas_call(
        functools.partial(attend_kernel, blocks=blocks, per_list=per_list),
        grid_spec=pltpu.PrefetchScalarGridSpec(
            num_scalar_prefetch=1,
            grid=(heads,),
            in_specs=[whole, whole, side, side],
            out_specs=[whole, whole, pl.BlockSpec((1, 2 * CROSS, BLOCK, 128), lambda h, *_: (h, 0, 0, 0))],
            scratch_shapes=[
                pltpu.VMEM((window, BLOCK, 128), bf16),
                pltpu.VMEM((window, 128, BLOCK), bf16),
                pltpu.VMEM((window, BLOCK, 128), f32),
                pltpu.VMEM((per_list, BLOCK, 2 * BLOCK), f32),
                pltpu.VMEM((per_list, BLOCK, 2 * BLOCK), bf16),
            ],
        ),
        out_shape=[
            jax.ShapeDtypeStruct((16, heads, rows, 128), bf16),
            jax.ShapeDtypeStruct((16, heads, rows, 128), bf16),
            jax.ShapeDtypeStruct((heads, 2 * CROSS, BLOCK, 128), bf16),
        ],
        compiler_params=pltpu.CompilerParams(vmem_limit_bytes=56 << 20),
        name="attend",
    )(ids.reshape(-1), kv, qg, prev, nxt)


def fix_kernel(asked_ref, dkv_ref, back_ref, out_ref):
    out_ref[...] = dkv_ref[...]
    for c in range(2 * CROSS):
        block = asked_ref[c]
        row = pl.multiple_of((block % 2) * BLOCK, BLOCK)
        here = (block // 2, 0, pl.ds(row, BLOCK))
        term = out_ref[here].astype(jnp.float32) + back_ref[0, c].astype(jnp.float32)
        out_ref[here] = term.astype(out_ref.dtype)


def fix(asked, dkv, back):
    heads, rows = dkv.shape[1:3]
    whole = pl.BlockSpec((16, 1, rows, 128), lambda h, *_: (0, h, 0, 0))
    return pl.pallas_call(
        fix_kernel,
        grid_spec=pltpu.PrefetchScalarGridSpec(
            num_scalar_prefetch=1,
            grid=(heads,),
            in_specs=[whole, pl.BlockSpec((1, 2 * CROSS, BLOCK, 128), lambda h, *_: (h, 0, 0, 0))],
            out_specs=whole,
        ),
        out_shape=jax.ShapeDtypeStruct(dkv.shape, dkv.dtype),
        name="fix",
    )(asked, dkv, back)


def first_hits(pattern, base, blocks):
    ids = jnp.arange(blocks, dtype=jnp.int32)
    hits = jnp.any(pattern.reshape(-1)[:, None] == (base + ids)[None, :], axis=0)
    rank = jnp.sum(jnp.where(ids[None, :] <= ids[:, None], hits[None, :].astype(jnp.int32), 0), axis=1)
    slots = jnp.arange(CROSS, dtype=jnp.int32)
    chosen = hits[None, :] & (rank[None, :] == slots[:, None] + 1)
    return jnp.sum(jnp.where(chosen, ids[None, :], 0), axis=1)


def local(query, key, value, d_out, pattern):
    heads, blocks, per_list = pattern.shape
    own_base = lax.axis_index("slab") * blocks
    need_prev = first_hits(pattern, own_base - blocks, blocks)
    need_next = first_hits(pattern, own_base + blocks, blocks)
    asked_next = from_behind(need_prev, "slab", -1)
    asked_prev = from_behind(need_next, "slab", 1)
    kv, qg = pack(query, key, value, d_out)
    kv = lax.all_to_all(kv, "seq", split_axis=0, concat_axis=0, tiled=True)
    qg = lax.all_to_all(qg, "seq", split_axis=0, concat_axis=0, tiled=True)
    slots = jnp.arange(CROSS, dtype=jnp.int32)
    pos_prev = jnp.sum(jnp.where(pattern[..., None] == own_base - blocks + need_prev, slots, 0), axis=-1)
    pos_next = jnp.sum(jnp.where(pattern[..., None] == own_base + blocks + need_next, slots, 0), axis=-1)
    relative = pattern - own_base
    ids = jnp.where(relative < 0, blocks + pos_prev, jnp.where(relative < blocks, relative, blocks + CROSS + pos_next))

    def taken(asked):
        return jnp.stack(
            [
                lax.dynamic_slice(kv, (asked[c] // 2, 0, (asked[c] % 2) * BLOCK, 0), (1, heads, BLOCK, 128))[0]
                for c in range(CROSS)
            ],
            axis=1,
        )

    prev = from_behind(taken(asked_next), "slab", 1)
    nxt = from_behind(taken(asked_prev), "slab", -1)
    og, dkv, cross = attend(ids, kv, qg, prev, nxt)
    og = lax.all_to_all(og, "seq", split_axis=0, concat_axis=0, tiled=True)
    back_later = from_behind(cross[:, :CROSS], "slab", -1)
    back_earlier = from_behind(cross[:, CROSS:], "slab", 1)
    dkv = fix(jnp.concatenate([asked_next, asked_prev]), dkv, jnp.concatenate([back_later, back_earlier], axis=1))
    dkv = lax.all_to_all(dkv, "seq", split_axis=0, concat_axis=0, tiled=True)
    return tuple(unpack(og, dkv))


def solution(mesh):
    rows = P(("slab", "seq"), None)
    return jax.shard_map(
        local,
        mesh=mesh,
        in_specs=(rows, rows, rows, rows, P("seq", "slab", None)),
        out_specs=(rows, rows, rows, rows),
        check_vma=False,
    )
```

```python
import functools

import jax
import jax.numpy as jnp
from jax import lax
from jax.experimental import pallas as pl
from jax.experimental.pallas import tpu as pltpu
from jax.sharding import PartitionSpec as P

CROSS = 4
HDIM = 64
BLOCK = 128
SCALE = HDIM**-0.5
PEERS = 16
STEP = 7
MESH = pl.DeviceIdType.MESH
SPREAD = ((0, 1), (1, 0), (0, 3), (3, 0), (1, 1), (3, 3), (1, 3), (3, 1), (0, 2), (2, 0), (1, 2), (2, 1), (3, 2), (2, 3), (2, 2))


def from_behind(x, axis, by):
    count = lax.axis_size(axis)
    pairs = [(i, i + by) for i in range(count) if 0 <= i + by < count]
    return lax.ppermute(x, axis, pairs)


def slot_of(dz, dx):
    return ((dz % 4) * 4 + dx % 4) * STEP % PEERS


def pack_kernel(q_ref, k_ref, v_ref, g_ref, kv_ref, qg_ref):
    for t in range(3):
        cols = slice(128 * t, 128 * t + 128)
        q, k, v, g = q_ref[:, cols], k_ref[:, cols], v_ref[:, cols], g_ref[:, cols]
        q = q * jnp.asarray(SCALE, q.dtype)
        for i in range(2):
            head = 2 * t + i
            half = slice(64 * i, 64 * i + 64)
            kv = jnp.concatenate([k[:, half], v[:, half]], axis=1)
            qg = jnp.concatenate([q[:, half], g[:, half]], axis=1)
            for part in range(2):
                rows = slice(BLOCK * part, BLOCK * part + BLOCK)
                kv_ref[head // 3, head % 3, part] = kv[rows]
                qg_ref[head // 3, head % 3, part] = qg[rows]


def pack(q, k, v, g):
    rows = q.shape[0]
    spec = pl.BlockSpec((rows, 384), lambda i: (0, i))
    out = jax.ShapeDtypeStruct((PEERS, 3, 2, BLOCK, 128), q.dtype)
    out_spec = pl.BlockSpec((2, 3, 2, BLOCK, 128), lambda i: (i, 0, 0, 0, 0))
    return pl.pallas_call(
        pack_kernel,
        grid=(8,),
        in_specs=[spec] * 4,
        out_specs=[out_spec] * 2,
        out_shape=[out] * 2,
        cost_estimate=pl.CostEstimate(flops=0, bytes_accessed=12 << 20, transcendentals=0),
        name="pack",
    )(q, k, v, g)


def unpack_kernel(slots_ref, og0_ref, og1_ref, kv0_ref, kv1_ref, o_ref, dq_ref, dk_ref, dv_ref):
    og_refs, kv_refs = (og0_ref, og1_ref), (kv0_ref, kv1_ref)
    for t in range(3):
        cols = slice(128 * t, 128 * t + 128)
        a, b = 2 * t, 2 * t + 1
        for part in range(2):
            rows = slice(BLOCK * part, BLOCK * part + BLOCK)
            og_a, og_b = og_refs[a // 3][a % 3, 0, part], og_refs[b // 3][b % 3, 0, part]
            kv_a, kv_b = kv_refs[a // 3][a % 3, 0, part], kv_refs[b // 3][b % 3, 0, part]
            dq_ref[rows, cols] = jnp.concatenate([og_a[:, :64], og_b[:, :64]], axis=1)
            o_ref[rows, cols] = jnp.concatenate([og_a[:, 64:], og_b[:, 64:]], axis=1)
            dk_ref[rows, cols] = jnp.concatenate([kv_a[:, :64], kv_b[:, :64]], axis=1)
            dv_ref[rows, cols] = jnp.concatenate([kv_a[:, 64:], kv_b[:, 64:]], axis=1)


def unpack(slots, og, kv):
    def spec(which):
        return pl.BlockSpec((3, 1, 2, BLOCK, 128), lambda i, slots: (0, slots[2 * i + which], 0, 0, 0))

    rows = 2 * BLOCK
    out_spec = pl.BlockSpec((rows, 384), lambda i, slots: (0, i))
    out = jax.ShapeDtypeStruct((rows, 3072), og.dtype)
    return pl.pallas_call(
        unpack_kernel,
        grid_spec=pltpu.PrefetchScalarGridSpec(
            num_scalar_prefetch=1,
            grid=(8,),
            in_specs=[spec(0), spec(1), spec(0), spec(1)],
            out_specs=[out_spec] * 4,
        ),
        out_shape=[out] * 4,
        cost_estimate=pl.CostEstimate(flops=0, bytes_accessed=12 << 20, transcendentals=0),
        name="unpack",
    )(slots, og, og, kv, kv)


def nt(a, b):
    return lax.dot_general(a, b, (((1,), (1,)), ((), ())), preferred_element_type=jnp.float32)


def fused_kernel(
    tab_ref, kv_src, qg_src, og_out, dkv_out,
    kvin, qgin, kvx, stage, kvw, kvt, terms, seg, ogs, dks, sums, back, near, sd0, sd1, ex0, ex1,
    in_send, in_recv, in_self, x_send, x_recv, b_send, b_recv, o_send, o_recv, o_self,
    *, heads, blocks, per_list,
):
    bf16, f32 = jnp.bfloat16, jnp.float32
    me, slab = lax.axis_index("seq"), lax.axis_index("slab")
    slabs = lax.axis_size("slab")
    z, x = me // 4, me % 4
    entries = blocks * per_list
    window = blocks + 2 * CROSS
    at_perm = heads * entries
    at_keep = 2 * at_perm
    at_last = 3 * at_perm
    at_asked = at_last + heads * window
    at_later = at_asked + 2 * CROSS
    at_earlier = at_later + blocks
    after = {"slab": (slab + 1) % slabs}
    before = {"slab": (slab + slabs - 1) % slabs}

    def peer(dz, dx):
        return (z + dz) % 4 * 4 + (x + dx) % 4

    def remote(src, dst, send, recv, device):
        return pltpu.make_async_remote_copy(
            src_ref=src, dst_ref=dst, send_sem=send, recv_sem=recv, device_id=device, device_id_type=MESH
        )

    barrier = pltpu.get_barrier_semaphore()
    for dz, dx in SPREAD:
        pl.semaphore_signal(barrier, 1, device_id={"seq": peer(dz, dx)}, device_id_type=MESH)
    for device in (after, before):
        pl.semaphore_signal(barrier, 1, device_id=device, device_id_type=MESH)
    pl.semaphore_wait(barrier, len(SPREAD) + 2)

    inputs = ((kv_src, kvin), (qg_src, qgin))
    for h in range(heads):
        for t, (src, dst) in enumerate(inputs):
            pltpu.make_async_copy(src.at[me, h], dst.at[h, pl.ds(0, 2)], in_self.at[t, h]).start()
            for dz, dx in SPREAD:
                there = dst.at[h, pl.ds(2 * slot_of(-dz, -dx), 2)]
                to = peer(dz, dx)
                remote(src.at[to, h], there, in_send.at[t, h], in_recv.at[t, h], {"seq": to}).start()

    def arrived(t, h):
        src, dst = inputs[t]
        pltpu.make_async_copy(src.at[me, h], dst.at[h, pl.ds(0, 2)], in_self.at[t, h]).wait()
        rest = dst.at[h, pl.ds(2, blocks - 2)]
        pltpu.make_async_copy(rest, rest, in_recv.at[t, h]).wait()

    def crossing(h, side):
        return remote(
            stage.at[h, pl.ds(CROSS * side, CROSS)], kvx.at[h, pl.ds(CROSS * side, CROSS)],
            x_send.at[h, side], x_recv.at[h, side], (after, before)[side],
        )

    def returning(h, side):
        return remote(
            sums.at[h, pl.ds(CROSS * side, CROSS)], back.at[h, pl.ds(CROSS * side, CROSS)],
            b_send.at[h, side], b_recv.at[h, side], (before, after)[side],
        )

    def open_window(h):
        arrived(0, h)

        @pl.loop(0, blocks)
        def _(w):
            kvw[w] = kvin[h, w]

        for c in range(2 * CROSS):
            stage[h, c] = kvw[tab_ref[at_asked + c]]

        @pl.loop(0, blocks)
        def _(w):
            kvt[w] = kvin[h, w].T

        for side in range(2):
            crossing(h, side).start()

    seg[entries] = jnp.zeros((BLOCK, 128), bf16)
    near[2 * CROSS] = jnp.zeros((BLOCK, 128), bf16)
    left = lax.broadcasted_iota(jnp.int32, (BLOCK, 128), 1) < HDIM
    open_window(0)

    def output(src, dst, t, h, p):
        rel = p * STEP % PEERS
        dz, dx = rel // 4, rel % 4
        there = slot_of(4 - dz, 4 - dx)
        return remote(src.at[h, pl.ds(2 * p, 2)], dst.at[h, there], o_send.at[t, h], o_recv.at[t, h], {"seq": peer(dz, dx)})

    def output_self(src, dst, t, h):
        return pltpu.make_async_copy(src.at[h, pl.ds(0, 2)], dst.at[h, 0], o_self.at[t, h])

    @pl.loop(0, heads)
    def _(h):
        for side in range(2):
            crossing(h, side).wait_recv()
        for c in range(2 * CROSS):
            block = kvx[h, c]
            kvw[blocks + c] = block
            kvt[blocks + c] = block.T
        arrived(1, h)

        @pl.loop(0, blocks // 2)
        def _(p):
            @pl.when(p == 1)
            def _():
                output_self(ogs, og_out, 0, h).start()

            @pl.when(p > 1)
            def _():
                output(ogs, og_out, 0, h, p - 1).start()

            pairs = []
            for half, (sd, ex) in enumerate(((sd0, ex0), (sd1, ex1))):
                b = 2 * p + half
                qg = qgin[h, b]
                zero = jnp.zeros_like(qg)
                both = jnp.concatenate([jnp.where(left, qg, zero), jnp.where(left, zero, qg)], axis=0)
                base = (h * blocks + b) * per_list
                ids = [tab_ref[base + j] for j in range(per_list)]
                top = None
                for j in range(per_list):
                    pair = nt(kvw[ids[j]], both)
                    sd[j] = pair
                    part = jnp.max(pair[:, :BLOCK].reshape(16, 8, BLOCK), axis=0)
                    top = part if top is None else jnp.maximum(top, part)
                pairs.append((b, sd, ex, both, ids, jnp.max(top, axis=0, keepdims=True)))
            for b, sd, ex, both, ids, row_max in pairs:
                total = jnp.zeros((8, BLOCK), f32)
                mixed = jnp.zeros((8, BLOCK), f32)
                for j in range(per_list):
                    e = jnp.exp(sd[j, :, :BLOCK] - row_max)
                    sd[j, :, :BLOCK] = e
                    ex[j, :, BLOCK:] = e.astype(bf16)
                    total += jnp.sum(e.reshape(16, 8, BLOCK), axis=0)
                    mixed += jnp.sum((e * sd[j, :, BLOCK:]).reshape(16, 8, BLOCK), axis=0)
                inverse = 1.0 / jnp.sum(total, axis=0, keepdims=True)
                correction = jnp.sum(mixed, axis=0, keepdims=True) * inverse
                for j in range(per_list):
                    ex[j, :, :BLOCK] = (sd[j, :, :BLOCK] * (sd[j, :, BLOCK:] - correction)).astype(bf16)
                out = jnp.zeros((128, 2 * BLOCK), f32)
                for j in range(0, per_list, 2):
                    lhs = jnp.concatenate([kvt[ids[j]], kvt[ids[j + 1]]], axis=1)
                    rhs = ex[j : j + 2].reshape(2 * BLOCK, 2 * BLOCK)
                    out += jnp.dot(lhs, rhs, preferred_element_type=f32)
                outs = jnp.concatenate([out[:HDIM, :BLOCK] * (inverse * SCALE), out[HDIM:, BLOCK:] * inverse], axis=0)
                ogs[h, b] = outs.T.astype(bf16)
                column = jnp.broadcast_to(inverse, (BLOCK, BLOCK)).T
                scaled = (both.astype(f32) * jnp.concatenate([column, column], axis=0)).astype(bf16)
                for j in range(per_list):
                    terms[b * per_list + j] = jnp.dot(ex[j], scaled, preferred_element_type=f32)

        @pl.when(h + 1 < heads)
        def _():
            open_window(h + 1)

        output(ogs, og_out, 0, h, blocks // 2 - 1).start()

        def running(t, acc):
            keep = tab_ref[at_keep + h * entries + t].astype(f32)
            acc = acc * keep + terms[tab_ref[at_perm + h * entries + t]]
            seg[t] = acc.astype(bf16)
            return acc

        lax.fori_loop(0, entries, running, jnp.zeros((BLOCK, 128), f32))
        last = at_last + h * window
        for c in range(2 * CROSS):
            sums[h, c] = seg[tab_ref[last + blocks + c]]
        for side in range(2):
            returning(h, side).start()
        for side in range(2):
            returning(h, side).wait_recv()
        for c in range(2 * CROSS):
            near[c] = back[h, c]

        @pl.loop(0, blocks)
        def _(w):
            total = seg[tab_ref[last + w]].astype(f32)
            total += near[tab_ref[at_later + w]].astype(f32)
            total += near[tab_ref[at_earlier + w]].astype(f32)
            dks[h, w] = total.astype(bf16)

        output_self(dks, dkv_out, 1, h).start()

        @pl.loop(1, blocks // 2)
        def _(p):
            output(dks, dkv_out, 1, h, p).start()

    for h in range(heads):
        for t, (src, dst) in enumerate(inputs):
            rest = dst.at[h, pl.ds(2, blocks - 2)]
            pltpu.make_async_copy(rest, rest, in_send.at[t, h]).wait()
        for side in range(2):
            crossing(h, side).wait_send()
            returning(h, side).wait_send()
        for t, (src, dst) in enumerate(((ogs, og_out), (dks, dkv_out))):
            output_self(src, dst, t, h).wait()
            rest = src.at[h, pl.ds(2, blocks - 2)]
            pltpu.make_async_copy(rest, rest, o_send.at[t, h]).wait()
            landed = dst.at[h, pl.ds(1, PEERS - 1)]
            pltpu.make_async_copy(landed, landed, o_recv.at[t, h]).wait()


def fused(tab, kv, qg, heads, blocks, per_list):
    f32, bf16 = jnp.float32, jnp.bfloat16
    window = blocks + 2 * CROSS
    entries = blocks * per_list
    block = (BLOCK, 128)
    sems = pltpu.SemaphoreType.DMA
    out = jax.ShapeDtypeStruct((heads, PEERS, 2, BLOCK, 128), bf16)
    any_spec = pl.BlockSpec(memory_space=pl.ANY)
    return pl.pallas_call(
        functools.partial(fused_kernel, heads=heads, blocks=blocks, per_list=per_list),
        in_specs=[pl.BlockSpec(memory_space=pltpu.SMEM), any_spec, any_spec],
        out_specs=[any_spec, any_spec],
        out_shape=[out, out],
        scratch_shapes=[
            pltpu.VMEM((heads, blocks, *block), bf16),
            pltpu.VMEM((heads, blocks, *block), bf16),
            pltpu.VMEM((heads, 2 * CROSS, *block), bf16),
            pltpu.VMEM((heads, 2 * CROSS, *block), bf16),
            pltpu.VMEM((window, *block), bf16),
            pltpu.VMEM((window, *block), bf16),
            pltpu.VMEM((entries, *block), f32),
            pltpu.VMEM((entries + 1, *block), bf16),
            pltpu.VMEM((heads, blocks, *block), bf16),
            pltpu.VMEM((heads, blocks, *block), bf16),
            pltpu.VMEM((heads, 2 * CROSS, *block), bf16),
            pltpu.VMEM((heads, 2 * CROSS, *block), bf16),
            pltpu.VMEM((2 * CROSS + 1, *block), bf16),
            pltpu.VMEM((per_list, BLOCK, 2 * BLOCK), f32),
            pltpu.VMEM((per_list, BLOCK, 2 * BLOCK), f32),
            pltpu.VMEM((per_list, BLOCK, 2 * BLOCK), bf16),
            pltpu.VMEM((per_list, BLOCK, 2 * BLOCK), bf16),
        ]
        + [sems((2, heads))] * 3
        + [sems((heads, 2))] * 4
        + [sems((2, heads))] * 3,
        compiler_params=pltpu.CompilerParams(
            collective_id=0, has_side_effects=True, vmem_limit_bytes=60 << 20
        ),
        name="fused",
    )(tab, kv, qg)


def first_hits(pattern, base, blocks):
    ids = jnp.arange(blocks, dtype=jnp.int32)
    hits = jnp.any(pattern.reshape(-1)[:, None] == (base + ids)[None, :], axis=0)
    rank = jnp.sum(jnp.where(ids[None, :] <= ids[:, None], hits[None, :].astype(jnp.int32), 0), axis=1)
    slots = jnp.arange(CROSS, dtype=jnp.int32)
    chosen = hits[None, :] & (rank[None, :] == slots[:, None] + 1)
    return jnp.sum(jnp.where(chosen, ids[None, :], 0), axis=1)


def local(query, key, value, d_out, pattern):
    heads, blocks, per_list = pattern.shape
    i32 = jnp.int32
    own_base = lax.axis_index("slab") * blocks
    me = lax.axis_index("seq")
    z, x = me // 4, me % 4
    need_prev = first_hits(pattern, own_base - blocks, blocks)
    need_next = first_hits(pattern, own_base + blocks, blocks)
    asked_next = from_behind(need_prev, "slab", -1)
    asked_prev = from_behind(need_next, "slab", 1)
    kv, qg = pack(query, key, value, d_out)

    def place(block):
        source = block // 2
        return 2 * slot_of(source // 4 - z + 4, source % 4 - x + 4) + block % 2

    slots = jnp.arange(CROSS, dtype=i32)
    pos_prev = jnp.min(jnp.where(pattern[..., None] == own_base - blocks + need_prev, slots, CROSS - 1), axis=-1)
    pos_next = jnp.min(jnp.where(pattern[..., None] == own_base + blocks + need_next, slots, CROSS - 1), axis=-1)
    relative = pattern - own_base
    ids = jnp.where(
        relative < 0, blocks + pos_prev, jnp.where(relative < blocks, place(relative), blocks + CROSS + pos_next)
    )
    every = jnp.arange(blocks, dtype=i32)
    where_to = place(every)
    ids = jnp.sum(jnp.where((where_to[None, :] == every[:, None])[None, :, :, None], ids[:, None], 0), axis=2)
    flat = ids.reshape(heads, -1)
    entries = blocks * per_list
    number = jnp.arange(entries, dtype=i32)
    order = flat * entries + number
    rank = jnp.sum((order[:, None, :] < order[:, :, None]).astype(i32), axis=2)
    lands = rank[:, None, :] == number[None, :, None]
    perm = jnp.sum(jnp.where(lands, number, 0), axis=2)
    ranked = jnp.sum(jnp.where(lands, flat[:, None, :], 0), axis=2)
    keep = jnp.concatenate([jnp.zeros((heads, 1), i32), (ranked[:, 1:] == ranked[:, :-1]).astype(i32)], axis=1)
    spots = jnp.arange(blocks + 2 * CROSS, dtype=i32)
    upto = jnp.sum((flat[:, None, :] <= spots[None, :, None]).astype(i32), axis=2)
    held = jnp.any(flat[:, None, :] == spots[None, :, None], axis=2)
    last = jnp.where(held, upto - 1, entries)
    later, earlier = place(asked_next), place(asked_prev)

    def returned(asked, first):
        return jnp.min(jnp.where(asked[None, :] == every[:, None], first + slots, 2 * CROSS), axis=1)

    tab = jnp.concatenate(
        [a.reshape(-1) for a in (ids, perm, keep, last, later, earlier, returned(later, 0), returned(earlier, CROSS))]
    )
    og, dkv = fused(tab, kv, qg, heads, blocks, per_list)
    group = jnp.arange(PEERS, dtype=i32)
    return tuple(unpack(slot_of(group // 4 - z + 4, group % 4 - x + 4), og, dkv))


def solution(mesh):
    rows = P(("slab", "seq"), None)
    return jax.shard_map(
        local,
        mesh=mesh,
        in_specs=(rows, rows, rows, rows, P("seq", "slab", None)),
        out_specs=(rows, rows, rows, rows),
        check_vma=False,
    )
```

```python
import functools

import jax
import jax.numpy as jnp
from jax import lax
from jax.experimental import pallas as pl
from jax.experimental.pallas import tpu as pltpu
from jax.sharding import PartitionSpec as P

CROSS = 4
HDIM = 64
BLOCK = 128
SCALE = HDIM**-0.5
PEERS = 16
STEP = 7
MESH = pl.DeviceIdType.MESH
SPREAD = ((0, 1), (1, 0), (0, 3), (3, 0), (1, 1), (3, 3), (1, 3), (3, 1), (0, 2), (2, 0), (1, 2), (2, 1), (3, 2), (2, 3), (2, 2))


def slot_of(dz, dx):
    return ((dz % 4) * 4 + dx % 4) * STEP % PEERS


def unpack_kernel(slots_ref, og0_ref, og1_ref, kv0_ref, kv1_ref, o_ref, dq_ref, dk_ref, dv_ref):
    og_refs, kv_refs = (og0_ref, og1_ref), (kv0_ref, kv1_ref)
    for t in range(3):
        cols = slice(128 * t, 128 * t + 128)
        a, b = 2 * t, 2 * t + 1
        for part in range(2):
            rows = slice(BLOCK * part, BLOCK * part + BLOCK)
            og_a, og_b = og_refs[a // 3][a % 3, 0, part], og_refs[b // 3][b % 3, 0, part]
            kv_a, kv_b = kv_refs[a // 3][a % 3, 0, part], kv_refs[b // 3][b % 3, 0, part]
            dq_ref[rows, cols] = jnp.concatenate([og_a[:, :64], og_b[:, :64]], axis=1)
            o_ref[rows, cols] = jnp.concatenate([og_a[:, 64:], og_b[:, 64:]], axis=1)
            dk_ref[rows, cols] = jnp.concatenate([kv_a[:, :64], kv_b[:, :64]], axis=1)
            dv_ref[rows, cols] = jnp.concatenate([kv_a[:, 64:], kv_b[:, 64:]], axis=1)


def unpack(slots, og, kv):
    def spec(which):
        return pl.BlockSpec((3, 1, 2, BLOCK, 128), lambda i, slots: (0, slots[2 * i + which], 0, 0, 0))

    rows = 2 * BLOCK
    out_spec = pl.BlockSpec((rows, 384), lambda i, slots: (0, i))
    out = jax.ShapeDtypeStruct((rows, 3072), og.dtype)
    return pl.pallas_call(
        unpack_kernel,
        grid_spec=pltpu.PrefetchScalarGridSpec(
            num_scalar_prefetch=1,
            grid=(8,),
            in_specs=[spec(0), spec(1), spec(0), spec(1)],
            out_specs=[out_spec] * 4,
        ),
        out_shape=[out] * 4,
        cost_estimate=pl.CostEstimate(flops=0, bytes_accessed=12 << 20, transcendentals=0),
        name="unpack",
    )(slots, og, og, kv, kv)


def nt(a, b):
    return lax.dot_general(a, b, (((1,), (1,)), ((), ())), preferred_element_type=jnp.float32)


def turned(row, size):
    return jnp.broadcast_to(row, (size, size)).T


def plan(pat_ref, tab_ref, ask_ref, base, z, x, heads, blocks, per_list):
    i32 = jnp.int32
    entries = blocks * per_list

    def grid(rows, columns, dim):
        return lax.broadcasted_iota(i32, (rows, columns), dim)

    def total(picked, value):
        return jnp.sum(jnp.where(picked, value, 0), axis=0, keepdims=True)

    def place(block):
        source = block >> 1
        rel = ((((source >> 2) - z) & 3) << 2) + (((source & 3) - x) & 3)
        return (((rel * STEP) & (PEERS - 1)) << 1) + (block & 1)

    rows = []
    hits = [jnp.zeros((1, 128), i32), jnp.zeros((1, 128), i32)]
    spot = grid(entries, 128, 1)
    for h in range(heads):
        pattern = pat_ref[h]
        lane = grid(blocks, entries, 1)
        spread = jnp.zeros((blocks, entries), i32)
        for j in range(per_list):
            spread = jnp.where((lane & (per_list - 1)) == j, pattern[:, j : j + 1], spread)
        mine = (lane >> 3) == grid(blocks, entries, 0)
        rows.append(total(mine, spread) - base)
        column = turned(rows[h], entries)[:, :128]
        for side, shift in enumerate((-blocks, blocks)):
            found = (column == spot + shift) & (spot < blocks)
            hits[side] = jnp.maximum(hits[side], jnp.max(found.astype(i32), axis=0, keepdims=True))
    down, across = grid(128, 128, 0), grid(128, 128, 1)
    ranks = []
    for side in range(2):
        hit = turned(hits[side], 128)
        rank = turned(total(down <= across, hit), 128)
        ranks.append(rank)
        ask_ref[side, 0:1] = total((hit > 0) & (rank == across + 1), place(down))
        back = jnp.where(hit > 0, rank - 1 + CROSS * side, 2 * CROSS)
        ask_ref[side, 1:2] = total((place(down) == across) & (down < blocks), back)
    number = grid(1, entries, 1)
    order = grid(entries, entries, 1)
    for h in range(heads):
        row = rows[h]
        block = grid(128, entries, 0)
        column = [jnp.concatenate([rank, rank], axis=1) for rank in ranks]
        outside = [total(block == row + shift, column[side] - 1) for side, shift in enumerate((blocks, -blocks))]
        ids = jnp.where(
            row < 0, blocks + outside[0], jnp.where(row < blocks, place(row), blocks + CROSS + outside[1])
        )
        key = ids * entries + number
        rank = total(turned(key, entries) < key, 1)
        column, rank = turned(ids, entries), turned(rank, entries)
        lands = rank == order
        ranked = total(lands, column)
        ahead = total(rank + 1 == order, column)
        tab_ref[h, 0:1] = ids
        tab_ref[h, 1:2] = total(lands, grid(entries, entries, 0))
        tab_ref[h, 2:3] = jnp.where((ranked == ahead) & (number > 0), 1, 0)
        upto = total(column <= order, 1)
        held = total(column == order, 1)
        tab_ref[h, 3:4] = jnp.where(held > 0, upto - 1, entries)


def fused_kernel(
    pat_ref, q_src, k_src, v_src, g_src, og_out, dkv_out,
    raw_q, raw_k, raw_v, raw_g, tabv, tab, askv, gotv, got,
    kvin, qgin, kvx, stage, kvw, kvt, terms, seg, ogs, dks, sums, back, near, sd0, sd1, ex0, ex1,
    in_send, in_recv, in_self, x_send, x_recv, b_send, b_recv, o_send, o_recv, o_self,
    raw_sem, tab_sem, got_sem, a_send, a_recv,
    *, heads, blocks, per_list,
):
    bf16, f32 = jnp.bfloat16, jnp.float32
    me, slab = lax.axis_index("seq"), lax.axis_index("slab")
    slabs = lax.axis_size("slab")
    z, x = me // 4, me % 4
    entries = blocks * per_list
    after = {"slab": (slab + 1) % slabs}
    before = {"slab": (slab + slabs - 1) % slabs}

    def peer(dz, dx):
        return (z + dz) % 4 * 4 + (x + dx) % 4

    def remote(src, dst, send, recv, device):
        return pltpu.make_async_remote_copy(
            src_ref=src, dst_ref=dst, send_sem=send, recv_sem=recv, device_id=device, device_id_type=MESH
        )

    raws = ((k_src, raw_k), (v_src, raw_v), (q_src, raw_q), (g_src, raw_g))
    loads = [pltpu.make_async_copy(src, dst, raw_sem.at[i]) for i, (src, dst) in enumerate(raws)]
    for load in loads:
        load.start()
    barrier = pltpu.get_barrier_semaphore()
    for dz, dx in SPREAD:
        pl.semaphore_signal(barrier, 1, device_id={"seq": peer(dz, dx)}, device_id_type=MESH)
    for device in (after, before):
        pl.semaphore_signal(barrier, 1, device_id=device, device_id_type=MESH)
    pl.semaphore_wait(barrier, len(SPREAD) + 2)

    inputs = ((raw_k, raw_v, dks, kvin), (raw_q, raw_g, ogs, qgin))

    def input_self(t, h):
        return pltpu.make_async_copy(
            inputs[t][2].at[h, pl.ds(0, 2)], inputs[t][3].at[h, pl.ds(0, 2)], in_self.at[t, h]
        )

    def send_input(t, h, p):
        rel = p * STEP % PEERS
        dz, dx = rel // 4, rel % 4
        there = inputs[t][3].at[h, pl.ds(2 * slot_of(4 - dz, 4 - dx), 2)]
        src = inputs[t][2].at[h, pl.ds(2 * p, 2)]
        remote(src, there, in_send.at[t, h], in_recv.at[t, h], {"seq": peer(dz, dx)}).start()

    for h in range(heads):
        for t in range(2):
            if h == 0:
                loads[2 * t].wait()
                loads[2 * t + 1].wait()
            one, two, packed, _ = inputs[t]

            @pl.loop(0, PEERS)
            def _(p):
                rel = p * STEP % PEERS
                column = 3 * peer(rel // 4, rel % 4) + h
                lanes = pl.ds(pl.multiple_of(column // 2 * 128, 128), 128)

                for side in range(2):

                    @pl.when(column % 2 == side)
                    def _():
                        half = slice(HDIM * side, HDIM * side + HDIM)
                        for part in range(2):
                            rows = pl.ds(BLOCK * part, BLOCK)
                            a, b = one[rows, lanes], two[rows, lanes]
                            if t == 1:
                                a = a * jnp.asarray(SCALE, bf16)
                            packed[h, 2 * p + part] = jnp.concatenate([a[:, half], b[:, half]], axis=1)

                @pl.when(p == 1)
                def _():
                    input_self(t, h).start()

                @pl.when(p > 1)
                def _():
                    send_input(t, h, p - 1)

            send_input(t, h, PEERS - 1)

    def arrived(t, h):
        input_self(t, h).wait()
        rest = inputs[t][3].at[h, pl.ds(2, blocks - 2)]
        pltpu.make_async_copy(rest, rest, in_recv.at[t, h]).wait()

    def sent(t, h):
        rest = inputs[t][2].at[h, pl.ds(2, blocks - 2)]
        pltpu.make_async_copy(rest, rest, in_send.at[t, h]).wait()

    plan(pat_ref, tabv, askv, slab * blocks, z, x, heads, blocks, per_list)
    asking = [remote(askv.at[i], gotv.at[i], a_send.at[i], a_recv.at[i], (before, after)[i]) for i in range(2)]
    for ask in asking:
        ask.start()
    table = pltpu.make_async_copy(tabv, tab, tab_sem.at[0])
    table.start()
    for ask in asking:
        ask.wait()
    gotten = pltpu.make_async_copy(gotv, got, got_sem.at[0])
    gotten.start()
    table.wait()
    gotten.wait()

    def crossing(h, side):
        return remote(
            stage.at[h, pl.ds(CROSS * side, CROSS)], kvx.at[h, pl.ds(CROSS * side, CROSS)],
            x_send.at[h, side], x_recv.at[h, side], (after, before)[side],
        )

    def returning(h, side):
        return remote(
            sums.at[h, pl.ds(CROSS * side, CROSS)], back.at[h, pl.ds(CROSS * side, CROSS)],
            b_send.at[h, side], b_recv.at[h, side], (before, after)[side],
        )

    def open_window(h):
        arrived(0, h)

        @pl.loop(0, blocks)
        def _(w):
            kvw[w] = kvin[h, w]

        for c in range(2 * CROSS):
            stage[h, c] = kvw[got[c // CROSS, 0, c % CROSS]]

        @pl.loop(0, blocks)
        def _(w):
            kvt[w] = kvin[h, w].T

        for side in range(2):
            crossing(h, side).start()

    seg[entries] = jnp.zeros((BLOCK, 128), bf16)
    near[2 * CROSS] = jnp.zeros((BLOCK, 128), bf16)
    left = lax.broadcasted_iota(jnp.int32, (BLOCK, 128), 1) < HDIM
    open_window(0)

    def output(src, dst, t, h, p):
        rel = p * STEP % PEERS
        dz, dx = rel // 4, rel % 4
        there = slot_of(4 - dz, 4 - dx)
        return remote(src.at[h, pl.ds(2 * p, 2)], dst.at[h, there], o_send.at[t, h], o_recv.at[t, h], {"seq": peer(dz, dx)})

    def output_self(src, dst, t, h):
        return pltpu.make_async_copy(src.at[h, pl.ds(0, 2)], dst.at[h, 0], o_self.at[t, h])

    @pl.loop(0, heads)
    def _(h):
        for side in range(2):
            crossing(h, side).wait_recv()
        for c in range(2 * CROSS):
            block = kvx[h, c]
            kvw[blocks + c] = block
            kvt[blocks + c] = block.T
        arrived(1, h)
        sent(0, h)
        sent(1, h)

        @pl.loop(0, blocks // 2)
        def _(p):
            @pl.when(p == 1)
            def _():
                output_self(ogs, og_out, 0, h).start()

            @pl.when(p > 1)
            def _():
                output(ogs, og_out, 0, h, p - 1).start()

            rel = p * STEP % PEERS
            first = 2 * per_list * peer(rel // 4, rel % 4)
            pairs = []
            for half, (sd, ex) in enumerate(((sd0, ex0), (sd1, ex1))):
                b = 2 * p + half
                qg = qgin[h, b]
                zero = jnp.zeros_like(qg)
                both = jnp.concatenate([jnp.where(left, qg, zero), jnp.where(left, zero, qg)], axis=0)
                base = first + half * per_list
                ids = [tab[h, 0, base + j] for j in range(per_list)]
                top = None
                for j in range(per_list):
                    pair = nt(kvw[ids[j]], both)
                    sd[j] = pair
                    part = jnp.max(pair[:, :BLOCK].reshape(16, 8, BLOCK), axis=0)
                    top = part if top is None else jnp.maximum(top, part)
                pairs.append((b, base, sd, ex, both, ids, jnp.max(top, axis=0, keepdims=True)))
            for b, base, sd, ex, both, ids, row_max in pairs:
                total = jnp.zeros((8, BLOCK), f32)
                mixed = jnp.zeros((8, BLOCK), f32)
                for j in range(per_list):
                    e = jnp.exp(sd[j, :, :BLOCK] - row_max)
                    sd[j, :, :BLOCK] = e
                    ex[j, :, BLOCK:] = e.astype(bf16)
                    total += jnp.sum(e.reshape(16, 8, BLOCK), axis=0)
                    mixed += jnp.sum((e * sd[j, :, BLOCK:]).reshape(16, 8, BLOCK), axis=0)
                inverse = 1.0 / jnp.sum(total, axis=0, keepdims=True)
                correction = jnp.sum(mixed, axis=0, keepdims=True) * inverse
                for j in range(per_list):
                    ex[j, :, :BLOCK] = (sd[j, :, :BLOCK] * (sd[j, :, BLOCK:] - correction)).astype(bf16)
                out = jnp.zeros((128, 2 * BLOCK), f32)
                for j in range(0, per_list, 2):
                    lhs = jnp.concatenate([kvt[ids[j]], kvt[ids[j + 1]]], axis=1)
                    rhs = ex[j : j + 2].reshape(2 * BLOCK, 2 * BLOCK)
                    out += jnp.dot(lhs, rhs, preferred_element_type=f32)
                outs = jnp.concatenate([out[:HDIM, :BLOCK] * (inverse * SCALE), out[HDIM:, BLOCK:] * inverse], axis=0)
                ogs[h, b] = outs.T.astype(bf16)
                column = jnp.broadcast_to(inverse, (BLOCK, BLOCK)).T
                scaled = (both.astype(f32) * jnp.concatenate([column, column], axis=0)).astype(bf16)
                for j in range(per_list):
                    terms[base + j] = jnp.dot(ex[j], scaled, preferred_element_type=f32)

        @pl.when(h + 1 < heads)
        def _():
            open_window(h + 1)

        output(ogs, og_out, 0, h, blocks // 2 - 1).start()

        def running(t, acc):
            keep = tab[h, 2, t].astype(f32)
            acc = acc * keep + terms[tab[h, 1, t]]
            seg[t] = acc.astype(bf16)
            return acc

        lax.fori_loop(0, entries, running, jnp.zeros((BLOCK, 128), f32))
        for c in range(2 * CROSS):
            sums[h, c] = seg[tab[h, 3, blocks + c]]
        for side in range(2):
            returning(h, side).start()
        for side in range(2):
            returning(h, side).wait_recv()
        for c in range(2 * CROSS):
            near[c] = back[h, c]

        @pl.loop(0, blocks)
        def _(w):
            total = seg[tab[h, 3, w]].astype(f32)
            total += near[got[0, 1, w]].astype(f32)
            total += near[got[1, 1, w]].astype(f32)
            dks[h, w] = total.astype(bf16)

        output_self(dks, dkv_out, 1, h).start()

        @pl.loop(1, blocks // 2)
        def _(p):
            output(dks, dkv_out, 1, h, p).start()

    for h in range(heads):
        for side in range(2):
            crossing(h, side).wait_send()
            returning(h, side).wait_send()
        for t, (src, dst) in enumerate(((ogs, og_out), (dks, dkv_out))):
            output_self(src, dst, t, h).wait()
            rest = src.at[h, pl.ds(2, blocks - 2)]
            pltpu.make_async_copy(rest, rest, o_send.at[t, h]).wait()
            landed = dst.at[h, pl.ds(1, PEERS - 1)]
            pltpu.make_async_copy(landed, landed, o_recv.at[t, h]).wait()


def fused(pattern, q, k, v, g):
    heads, blocks, per_list = pattern.shape
    f32, bf16 = jnp.float32, jnp.bfloat16
    window = blocks + 2 * CROSS
    entries = blocks * per_list
    block = (BLOCK, 128)
    sems = pltpu.SemaphoreType.DMA
    out = jax.ShapeDtypeStruct((heads, PEERS, 2, BLOCK, 128), bf16)
    any_spec = pl.BlockSpec(memory_space=pl.ANY)
    return pl.pallas_call(
        functools.partial(fused_kernel, heads=heads, blocks=blocks, per_list=per_list),
        in_specs=[pl.BlockSpec(memory_space=pltpu.VMEM)] + [any_spec] * 4,
        out_specs=[any_spec, any_spec],
        out_shape=[out, out],
        scratch_shapes=[pltpu.VMEM(q.shape, bf16)] * 4
        + [
            pltpu.VMEM((heads, 8, entries), jnp.int32),
            pltpu.SMEM((heads, 8, entries), jnp.int32),
            pltpu.VMEM((2, 8, 128), jnp.int32),
            pltpu.VMEM((2, 8, 128), jnp.int32),
            pltpu.SMEM((2, 8, 128), jnp.int32),
            pltpu.VMEM((heads, blocks, *block), bf16),
            pltpu.VMEM((heads, blocks, *block), bf16),
            pltpu.VMEM((heads, 2 * CROSS, *block), bf16),
            pltpu.VMEM((heads, 2 * CROSS, *block), bf16),
            pltpu.VMEM((window, *block), bf16),
            pltpu.VMEM((window, *block), bf16),
            pltpu.VMEM((entries, *block), f32),
            pltpu.VMEM((entries + 1, *block), bf16),
            pltpu.VMEM((heads, blocks, *block), bf16),
            pltpu.VMEM((heads, blocks, *block), bf16),
            pltpu.VMEM((heads, 2 * CROSS, *block), bf16),
            pltpu.VMEM((heads, 2 * CROSS, *block), bf16),
            pltpu.VMEM((2 * CROSS + 1, *block), bf16),
            pltpu.VMEM((per_list, BLOCK, 2 * BLOCK), f32),
            pltpu.VMEM((per_list, BLOCK, 2 * BLOCK), f32),
            pltpu.VMEM((per_list, BLOCK, 2 * BLOCK), bf16),
            pltpu.VMEM((per_list, BLOCK, 2 * BLOCK), bf16),
        ]
        + [sems((2, heads))] * 3
        + [sems((heads, 2))] * 4
        + [sems((2, heads))] * 3
        + [sems((4,)), sems((1,)), sems((1,)), sems((2,)), sems((2,))],
        compiler_params=pltpu.CompilerParams(
            collective_id=0, has_side_effects=True, vmem_limit_bytes=60 << 20
        ),
        name="fused",
    )(pattern, q, k, v, g)


def local(query, key, value, d_out, pattern):
    me = lax.axis_index("seq")
    z, x = me // 4, me % 4
    og, dkv = fused(pattern, query, key, value, d_out)
    group = jnp.arange(PEERS, dtype=jnp.int32)
    return tuple(unpack(slot_of(group // 4 - z + 4, group % 4 - x + 4), og, dkv))


def solution(mesh):
    rows = P(("slab", "seq"), None)
    return jax.shard_map(
        local,
        mesh=mesh,
        in_specs=(rows, rows, rows, rows, P("seq", "slab", None)),
        out_specs=(rows, rows, rows, rows),
        check_vma=False,
    )
```

```python
import functools

import jax
import jax.numpy as jnp
from jax import lax
from jax.experimental import pallas as pl
from jax.experimental.pallas import tpu as pltpu
from jax.sharding import PartitionSpec as P

CROSS = 4
HDIM = 64
BLOCK = 128
SCALE = HDIM**-0.5
PEERS = 16
STEP = 7
MESH = pl.DeviceIdType.MESH
SPREAD = ((0, 1), (1, 0), (0, 3), (3, 0), (1, 1), (3, 3), (1, 3), (3, 1), (0, 2), (2, 0), (1, 2), (2, 1), (3, 2), (2, 3), (2, 2))


def slot_of(dz, dx):
    return ((dz % 4) * 4 + dx % 4) * STEP % PEERS


def unpack_kernel(og_src, kv_src, o_out, dq_out, dk_out, dv_out, og, kv, o_ref, dq_ref, dk_ref, dv_ref, in_sem, out_sem):
    me = lax.axis_index("seq")
    z, x = me // 4, me % 4
    loads = []
    for g in range(PEERS):
        slot = slot_of(g // 4 - z + 4, g % 4 - x + 4)
        pair = [
            pltpu.make_async_copy(src.at[:, slot], dst.at[g], in_sem.at[i, g])
            for i, (src, dst) in enumerate(((og_src, og), (kv_src, kv)))
        ]
        for load in pair:
            load.start()
        loads.append(pair)
    left = lax.broadcasted_iota(jnp.int32, (BLOCK, 128), 1) < HDIM
    stores = []
    for i in range(PEERS // 2):
        for g in (2 * i, 2 * i + 1):
            for load in loads[g]:
                load.wait()
        for t in range(3):
            cols = slice(384 * i + 128 * t, 384 * i + 128 * t + 128)
            a, b = 6 * i + 2 * t, 6 * i + 2 * t + 1
            for part in range(2):
                rows = slice(BLOCK * part, BLOCK * part + BLOCK)
                for src, low, high in ((og, dq_ref, o_ref), (kv, dk_ref, dv_ref)):
                    one, two = src[a // 3, a % 3, part], src[b // 3, b % 3, part]
                    low[rows, cols] = jnp.where(left, one, pltpu.roll(two, HDIM, 1))
                    high[rows, cols] = jnp.where(left, pltpu.roll(one, HDIM, 1), two)
        cols = slice(384 * i, 384 * i + 384)
        for n, (src, dst) in enumerate(((o_ref, o_out), (dq_ref, dq_out), (dk_ref, dk_out), (dv_ref, dv_out))):
            store = pltpu.make_async_copy(src.at[:, cols], dst.at[:, cols], out_sem.at[n, i])
            store.start()
            stores.append(store)
    for store in stores:
        store.wait()


def unpack(og, kv):
    rows = 2 * BLOCK
    any_spec = pl.BlockSpec(memory_space=pl.ANY)
    out = jax.ShapeDtypeStruct((rows, 3072), og.dtype)
    return pl.pallas_call(
        unpack_kernel,
        in_specs=[any_spec] * 2,
        out_specs=[any_spec] * 4,
        out_shape=[out] * 4,
        scratch_shapes=[pltpu.VMEM((PEERS, 3, 2, BLOCK, 128), og.dtype)] * 2
        + [pltpu.VMEM((rows, 3072), og.dtype)] * 4
        + [pltpu.SemaphoreType.DMA((2, PEERS)), pltpu.SemaphoreType.DMA((4, PEERS // 2))],
        name="unpack",
    )(og, kv)


def nt(a, b):
    return lax.dot_general(a, b, (((1,), (1,)), ((), ())), preferred_element_type=jnp.float32)


def turned(row, size):
    return jnp.broadcast_to(row, (size, size)).T


def plan(pat_ref, tab_ref, ask_ref, base, z, x, heads, blocks, per_list):
    i32 = jnp.int32
    entries = blocks * per_list

    def grid(rows, columns, dim):
        return lax.broadcasted_iota(i32, (rows, columns), dim)

    def total(picked, value):
        return jnp.sum(jnp.where(picked, value, 0), axis=0, keepdims=True)

    def place(block):
        source = block >> 1
        rel = ((((source >> 2) - z) & 3) << 2) + (((source & 3) - x) & 3)
        return (((rel * STEP) & (PEERS - 1)) << 1) + (block & 1)

    def turn(ids):
        return jnp.where(ids < blocks, ids + 2 * CROSS, ids - blocks)

    rows = []
    hits = [jnp.zeros((1, 128), i32), jnp.zeros((1, 128), i32)]
    spot = grid(entries, 128, 1)
    for h in range(heads):
        pattern = pat_ref[h]
        lane = grid(blocks, entries, 1)
        spread = jnp.zeros((blocks, entries), i32)
        for j in range(per_list):
            spread = jnp.where((lane & (per_list - 1)) == j, pattern[:, j : j + 1], spread)
        mine = (lane >> 3) == grid(blocks, entries, 0)
        rows.append(total(mine, spread) - base)
        column = turned(rows[h], entries)[:, :128]
        for side, shift in enumerate((-blocks, blocks)):
            found = (column == spot + shift) & (spot < blocks)
            hits[side] = jnp.maximum(hits[side], jnp.max(found.astype(i32), axis=0, keepdims=True))
    down, across = grid(128, 128, 0), grid(128, 128, 1)
    ranks = []
    for side in range(2):
        hit = turned(hits[side], 128)
        rank = turned(total(down <= across, hit), 128)
        ranks.append(rank)
        ask_ref[side, 0:1] = total((hit > 0) & (rank == across + 1), place(down))
        back = jnp.where(hit > 0, rank - 1 + CROSS * side, 2 * CROSS)
        ask_ref[side, 1:2] = total((place(down) == across) & (down < blocks), back)
    number = grid(1, entries, 1)
    order = grid(entries, entries, 1)
    for h in range(heads):
        row = rows[h]
        block = grid(128, entries, 0)
        column = [jnp.concatenate([rank, rank], axis=1) for rank in ranks]
        outside = [total(block == row + shift, column[side] - 1) for side, shift in enumerate((blocks, -blocks))]
        ids = jnp.where(
            row < 0, blocks + outside[0], jnp.where(row < blocks, place(row), blocks + CROSS + outside[1])
        )
        key = turn(ids) * entries + number
        rank = total(turned(key, entries) < key, 1)
        column, rank = turned(ids, entries), turned(rank, entries)
        lands = rank == order
        ranked = total(lands, column)
        ahead = total(rank + 1 == order, column)
        tab_ref[h, 0:1] = ids
        tab_ref[h, 1:2] = total(lands, grid(entries, entries, 0))
        tab_ref[h, 2:3] = jnp.where((ranked == ahead) & (number > 0), 1, 0)
        upto = total(turn(column) <= turn(order), 1)
        held = total(column == order, 1)
        tab_ref[h, 3:4] = jnp.where(held > 0, upto - 1, entries)


def fused_kernel(
    pat_src, q_src, k_src, v_src, g_src, og_out, dkv_out,
    pat_ref, raw_q, raw_k, raw_v, raw_g, tabv, tab, askv, gotv, got,
    kvin, qgin, kvx, stage, kvw, kvt, terms, seg, ogs, dks, sums, back, near, sd0, sd1, ex0, ex1,
    in_send, in_recv, in_self, x_send, x_recv, b_send, b_recv, o_send, o_recv, o_self,
    raw_sem, pat_sem, tab_sem, got_sem, a_send, a_recv, q_recv,
    *, heads, blocks, per_list,
):
    bf16, f32 = jnp.bfloat16, jnp.float32
    me, slab = lax.axis_index("seq"), lax.axis_index("slab")
    slabs = lax.axis_size("slab")
    z, x = me // 4, me % 4
    entries = blocks * per_list
    after = {"slab": (slab + 1) % slabs}
    before = {"slab": (slab + slabs - 1) % slabs}

    def peer(dz, dx):
        return (z + dz) % 4 * 4 + (x + dx) % 4

    def remote(src, dst, send, recv, device):
        return pltpu.make_async_remote_copy(
            src_ref=src, dst_ref=dst, send_sem=send, recv_sem=recv, device_id=device, device_id_type=MESH
        )

    raws = ((k_src, raw_k), (v_src, raw_v), (q_src, raw_q), (g_src, raw_g))
    loads = [pltpu.make_async_copy(src, dst, raw_sem.at[i]) for i, (src, dst) in enumerate(raws)]
    for load in loads:
        load.start()
    pattern = pltpu.make_async_copy(pat_src, pat_ref, pat_sem.at[0])
    pattern.start()
    barrier = pltpu.get_barrier_semaphore()
    for dz, dx in SPREAD:
        pl.semaphore_signal(barrier, 1, device_id={"seq": peer(dz, dx)}, device_id_type=MESH)
    for device in (after, before):
        pl.semaphore_signal(barrier, 1, device_id=device, device_id_type=MESH)
    pl.semaphore_wait(barrier, len(SPREAD) + 2)

    inputs = ((raw_k, raw_v, ogs, kvin), (raw_q, raw_g, dks, qgin))

    def input_self(t, h):
        return pltpu.make_async_copy(
            inputs[t][2].at[h, pl.ds(0, 2)], inputs[t][3].at[h, pl.ds(0, 2)], in_self.at[t, h]
        )

    def send_input(t, h, p):
        rel = p * STEP % PEERS
        dz, dx = rel // 4, rel % 4
        slot = slot_of(4 - dz, 4 - dx)
        there = inputs[t][3].at[h, pl.ds(2 * slot, 2)]
        src = inputs[t][2].at[h, pl.ds(2 * p, 2)]
        landing = in_recv.at[h] if t == 0 else q_recv.at[h, slot]
        remote(src, there, in_send.at[t, h], landing, {"seq": peer(dz, dx)}).start()

    for h in range(heads):
        for t in range(2):
            if h == 0:
                loads[2 * t].wait()
                loads[2 * t + 1].wait()
            one, two, packed, _ = inputs[t]

            @pl.loop(0, PEERS)
            def _(p):
                rel = p * STEP % PEERS
                column = 3 * peer(rel // 4, rel % 4) + h
                lanes = pl.ds(pl.multiple_of(column // 2 * 128, 128), 128)

                for side in range(2):

                    @pl.when(column % 2 == side)
                    def _():
                        half = slice(HDIM * side, HDIM * side + HDIM)
                        for part in range(2):
                            rows = pl.ds(BLOCK * part, BLOCK)
                            a, b = one[rows, lanes], two[rows, lanes]
                            if t == 1:
                                a = a * jnp.asarray(SCALE, bf16)
                            packed[h, 2 * p + part] = jnp.concatenate([a[:, half], b[:, half]], axis=1)

                @pl.when(p == 1)
                def _():
                    input_self(t, h).start()

                @pl.when(p > 1)
                def _():
                    send_input(t, h, p - 1)

            send_input(t, h, PEERS - 1)

    def arrived(h):
        input_self(0, h).wait()
        rest = kvin.at[h, pl.ds(2, blocks - 2)]
        pltpu.make_async_copy(rest, rest, in_recv.at[h]).wait()

    def sent(t, h):
        rest = inputs[t][2].at[h, pl.ds(2, blocks - 2)]
        pltpu.make_async_copy(rest, rest, in_send.at[t, h]).wait()

    pattern.wait()
    plan(pat_ref, tabv, askv, slab * blocks, z, x, heads, blocks, per_list)
    asking = [remote(askv.at[i], gotv.at[i], a_send.at[i], a_recv.at[i], (before, after)[i]) for i in range(2)]
    for ask in asking:
        ask.start()
    table = pltpu.make_async_copy(tabv, tab, tab_sem.at[0])
    table.start()
    for ask in asking:
        ask.wait()
    gotten = pltpu.make_async_copy(gotv, got, got_sem.at[0])
    gotten.start()
    table.wait()
    gotten.wait()

    def crossing(h, side):
        return remote(
            stage.at[h, pl.ds(CROSS * side, CROSS)], kvx.at[h, pl.ds(CROSS * side, CROSS)],
            x_send.at[h, side], x_recv.at[h, side], (after, before)[side],
        )

    def returning(h, side):
        return remote(
            sums.at[h, pl.ds(CROSS * side, CROSS)], back.at[h, pl.ds(CROSS * side, CROSS)],
            b_send.at[h, side], b_recv.at[h, side], (before, after)[side],
        )

    def open_window(h):
        arrived(h)

        @pl.loop(0, blocks)
        def _(w):
            kvw[w] = kvin[h, w]

        for c in range(2 * CROSS):
            stage[h, c] = kvw[got[c // CROSS, 0, c % CROSS]]

        @pl.loop(0, blocks)
        def _(w):
            kvt[w] = kvin[h, w].T

        for side in range(2):
            crossing(h, side).start()

    seg[entries] = jnp.zeros((BLOCK, 128), bf16)
    near[2 * CROSS] = jnp.zeros((BLOCK, 128), bf16)
    left = lax.broadcasted_iota(jnp.int32, (BLOCK, 128), 1) < HDIM
    open_window(0)

    def output(src, dst, t, h, p):
        rel = p * STEP % PEERS
        dz, dx = rel // 4, rel % 4
        there = slot_of(4 - dz, 4 - dx)
        return remote(src.at[h, pl.ds(2 * p, 2)], dst.at[h, there], o_send.at[t, h], o_recv.at[t, h], {"seq": peer(dz, dx)})

    def output_self(src, dst, t, h):
        return pltpu.make_async_copy(src.at[h, pl.ds(0, 2)], dst.at[h, 0], o_self.at[t, h])

    @pl.loop(0, heads)
    def _(h):
        for side in range(2):
            crossing(h, side).wait_recv()
        for c in range(2 * CROSS):
            block = kvx[h, c]
            kvw[blocks + c] = block
            kvt[blocks + c] = block.T
        sent(0, h)

        @pl.loop(0, blocks // 2)
        def _(p):
            @pl.when(p == 0)
            def _():
                input_self(1, h).wait()

            @pl.when(p > 0)
            def _():
                chunk = qgin.at[h, pl.ds(2 * p, 2)]
                pltpu.make_async_copy(chunk, chunk, q_recv.at[h, p]).wait()

            @pl.when(p == 1)
            def _():
                output_self(ogs, og_out, 0, h).start()

            @pl.when(p > 1)
            def _():
                output(ogs, og_out, 0, h, p - 1).start()

            rel = p * STEP % PEERS
            first = 2 * per_list * peer(rel // 4, rel % 4)
            pairs = []
            for half, (sd, ex) in enumerate(((sd0, ex0), (sd1, ex1))):
                b = 2 * p + half
                qg = qgin[h, b]
                zero = jnp.zeros_like(qg)
                both = jnp.concatenate([jnp.where(left, qg, zero), jnp.where(left, zero, qg)], axis=0)
                base = first + half * per_list
                ids = [tab[h, 0, base + j] for j in range(per_list)]
                top = None
                for j in range(per_list):
                    pair = nt(kvw[ids[j]], both)
                    sd[j] = pair
                    part = jnp.max(pair[:, :BLOCK].reshape(16, 8, BLOCK), axis=0)
                    top = part if top is None else jnp.maximum(top, part)
                pairs.append((b, base, sd, ex, both, ids, jnp.max(top, axis=0, keepdims=True)))
            for b, base, sd, ex, both, ids, row_max in pairs:
                total = jnp.zeros((8, BLOCK), f32)
                mixed = jnp.zeros((8, BLOCK), f32)
                for j in range(per_list):
                    e = jnp.exp(sd[j, :, :BLOCK] - row_max)
                    sd[j, :, :BLOCK] = e
                    ex[j, :, BLOCK:] = e.astype(bf16)
                    total += jnp.sum(e.reshape(16, 8, BLOCK), axis=0)
                    mixed += jnp.sum((e * sd[j, :, BLOCK:]).reshape(16, 8, BLOCK), axis=0)
                inverse = 1.0 / jnp.sum(total, axis=0, keepdims=True)
                correction = jnp.sum(mixed, axis=0, keepdims=True) * inverse
                for j in range(per_list):
                    ex[j, :, :BLOCK] = (sd[j, :, :BLOCK] * (sd[j, :, BLOCK:] - correction)).astype(bf16)
                out = jnp.zeros((128, 2 * BLOCK), f32)
                for j in range(0, per_list, 2):
                    lhs = jnp.concatenate([kvt[ids[j]], kvt[ids[j + 1]]], axis=1)
                    rhs = ex[j : j + 2].reshape(2 * BLOCK, 2 * BLOCK)
                    out += jnp.dot(lhs, rhs, preferred_element_type=f32)
                outs = jnp.concatenate([out[:HDIM, :BLOCK] * (inverse * SCALE), out[HDIM:, BLOCK:] * inverse], axis=0)
                ogs[h, b] = outs.T.astype(bf16)
                column = jnp.broadcast_to(inverse, (BLOCK, BLOCK)).T
                scaled = (both.astype(f32) * jnp.concatenate([column, column], axis=0)).astype(bf16)
                for j in range(per_list):
                    terms[base + j] = jnp.dot(ex[j], scaled, preferred_element_type=f32)

        @pl.when(h + 1 < heads)
        def _():
            open_window(h + 1)

        output(ogs, og_out, 0, h, blocks // 2 - 1).start()

        def running(t, acc):
            keep = tab[h, 2, t].astype(f32)
            acc = acc * keep + terms[tab[h, 1, t]]
            seg[t] = acc.astype(bf16)
            return acc

        acc = lax.fori_loop(0, entries // 2, running, jnp.zeros((BLOCK, 128), f32))
        for c in range(2 * CROSS):
            sums[h, c] = seg[tab[h, 3, blocks + c]]
        acc = lax.fori_loop(entries // 2, entries // 2 + 8, running, acc)
        for side in range(2):
            returning(h, side).start()
        lax.fori_loop(entries // 2 + 8, entries, running, acc)
        sent(1, h)
        for side in range(2):
            returning(h, side).wait_recv()
        for c in range(2 * CROSS):
            near[c] = back[h, c]

        @pl.loop(0, blocks // 2)
        def _(p):
            for half in range(2):
                w = 2 * p + half
                total = seg[tab[h, 3, w]].astype(f32)
                total += near[got[0, 1, w]].astype(f32)
                total += near[got[1, 1, w]].astype(f32)
                dks[h, w] = total.astype(bf16)

            @pl.when(p == 1)
            def _():
                output_self(dks, dkv_out, 1, h).start()

            @pl.when(p > 1)
            def _():
                output(dks, dkv_out, 1, h, p - 1).start()

        output(dks, dkv_out, 1, h, blocks // 2 - 1).start()

    for h in range(heads):
        for side in range(2):
            crossing(h, side).wait_send()
            returning(h, side).wait_send()
        for t, (src, dst) in enumerate(((ogs, og_out), (dks, dkv_out))):
            output_self(src, dst, t, h).wait()
            rest = src.at[h, pl.ds(2, blocks - 2)]
            pltpu.make_async_copy(rest, rest, o_send.at[t, h]).wait()
            landed = dst.at[h, pl.ds(1, PEERS - 1)]
            pltpu.make_async_copy(landed, landed, o_recv.at[t, h]).wait()


def fused(pattern, q, k, v, g):
    heads, blocks, per_list = pattern.shape
    f32, bf16 = jnp.float32, jnp.bfloat16
    window = blocks + 2 * CROSS
    entries = blocks * per_list
    block = (BLOCK, 128)
    sems = pltpu.SemaphoreType.DMA
    out = jax.ShapeDtypeStruct((heads, PEERS, 2, BLOCK, 128), bf16)
    any_spec = pl.BlockSpec(memory_space=pl.ANY)
    return pl.pallas_call(
        functools.partial(fused_kernel, heads=heads, blocks=blocks, per_list=per_list),
        in_specs=[any_spec] * 5,
        out_specs=[any_spec, any_spec],
        out_shape=[out, out],
        scratch_shapes=[pltpu.VMEM(pattern.shape, jnp.int32)]
        + [pltpu.VMEM(q.shape, bf16)] * 4
        + [
            pltpu.VMEM((heads, 8, entries), jnp.int32),
            pltpu.SMEM((heads, 8, entries), jnp.int32),
            pltpu.VMEM((2, 8, 128), jnp.int32),
            pltpu.VMEM((2, 8, 128), jnp.int32),
            pltpu.SMEM((2, 8, 128), jnp.int32),
            pltpu.VMEM((heads, blocks, *block), bf16),
            pltpu.VMEM((heads, blocks, *block), bf16),
            pltpu.VMEM((heads, 2 * CROSS, *block), bf16),
            pltpu.VMEM((heads, 2 * CROSS, *block), bf16),
            pltpu.VMEM((window, *block), bf16),
            pltpu.VMEM((window, *block), bf16),
            pltpu.VMEM((entries, *block), f32),
            pltpu.VMEM((entries + 1, *block), bf16),
            pltpu.VMEM((heads, blocks, *block), bf16),
            pltpu.VMEM((heads, blocks, *block), bf16),
            pltpu.VMEM((heads, 2 * CROSS, *block), bf16),
            pltpu.VMEM((heads, 2 * CROSS, *block), bf16),
            pltpu.VMEM((2 * CROSS + 1, *block), bf16),
            pltpu.VMEM((per_list, BLOCK, 2 * BLOCK), f32),
            pltpu.VMEM((per_list, BLOCK, 2 * BLOCK), f32),
            pltpu.VMEM((per_list, BLOCK, 2 * BLOCK), bf16),
            pltpu.VMEM((per_list, BLOCK, 2 * BLOCK), bf16),
        ]
        + [sems((2, heads)), sems((heads,)), sems((2, heads))]
        + [sems((heads, 2))] * 4
        + [sems((2, heads))] * 3
        + [sems((4,)), sems((1,)), sems((1,)), sems((1,)), sems((2,)), sems((2,)), sems((heads, PEERS))],
        compiler_params=pltpu.CompilerParams(
            collective_id=0, has_side_effects=True, vmem_limit_bytes=60 << 20
        ),
        name="fused",
    )(pattern, q, k, v, g)


def local(query, key, value, d_out, pattern):
    og, dkv = fused(pattern, query, key, value, d_out)
    return tuple(unpack(og, dkv))


def solution(mesh):
    rows = P(("slab", "seq"), None)
    return jax.shard_map(
        local,
        mesh=mesh,
        in_specs=(rows, rows, rows, rows, P("seq", "slab", None)),
        out_specs=(rows, rows, rows, rows),
        check_vma=False,
    )
```

```python
import functools

import jax
import jax.numpy as jnp
from jax import lax
from jax.experimental import pallas as pl
from jax.experimental.pallas import tpu as pltpu
from jax.sharding import PartitionSpec as P

CROSS = 4
HDIM = 64
BLOCK = 128
SCALE = HDIM**-0.5
PEERS = 16
STEP = 7
MESH = pl.DeviceIdType.MESH
SPREAD = ((0, 1), (1, 0), (0, 3), (3, 0), (1, 1), (3, 3), (1, 3), (3, 1), (0, 2), (2, 0), (1, 2), (2, 1), (3, 2), (2, 3), (2, 2))


def slot_of(dz, dx):
    return ((dz % 4) * 4 + dx % 4) * STEP % PEERS


def unpack_kernel(og_src, kv_src, o_out, dq_out, dk_out, dv_out, og, kv, o_ref, dq_ref, dk_ref, dv_ref, in_sem, out_sem):
    me = lax.axis_index("seq")
    z, x = me // 4, me % 4
    loads = []
    for g in range(PEERS):
        slot = slot_of(g // 4 - z + 4, g % 4 - x + 4)
        pair = [
            pltpu.make_async_copy(src.at[:, slot], dst.at[g], in_sem.at[i, g])
            for i, (src, dst) in enumerate(((og_src, og), (kv_src, kv)))
        ]
        for load in pair:
            load.start()
        loads.append(pair)
    left = lax.broadcasted_iota(jnp.int32, (BLOCK, 128), 1) < HDIM
    stores = []
    for i in range(PEERS // 2):
        for g in (2 * i, 2 * i + 1):
            for load in loads[g]:
                load.wait()
        for t in range(3):
            cols = slice(384 * i + 128 * t, 384 * i + 128 * t + 128)
            a, b = 6 * i + 2 * t, 6 * i + 2 * t + 1
            for part in range(2):
                rows = slice(BLOCK * part, BLOCK * part + BLOCK)
                for src, low, high in ((og, dq_ref, o_ref), (kv, dk_ref, dv_ref)):
                    one, two = src[a // 3, a % 3, part], src[b // 3, b % 3, part]
                    low[rows, cols] = jnp.where(left, one, pltpu.roll(two, HDIM, 1))
                    high[rows, cols] = jnp.where(left, pltpu.roll(one, HDIM, 1), two)
        cols = slice(384 * i, 384 * i + 384)
        for n, (src, dst) in enumerate(((o_ref, o_out), (dq_ref, dq_out), (dk_ref, dk_out), (dv_ref, dv_out))):
            store = pltpu.make_async_copy(src.at[:, cols], dst.at[:, cols], out_sem.at[n, i])
            store.start()
            stores.append(store)
    for store in stores:
        store.wait()


def unpack(og, kv):
    rows = 2 * BLOCK
    any_spec = pl.BlockSpec(memory_space=pl.ANY)
    out = jax.ShapeDtypeStruct((rows, 3072), og.dtype)
    return pl.pallas_call(
        unpack_kernel,
        in_specs=[any_spec] * 2,
        out_specs=[any_spec] * 4,
        out_shape=[out] * 4,
        scratch_shapes=[pltpu.VMEM((PEERS, 3, 2, BLOCK, 128), og.dtype)] * 2
        + [pltpu.VMEM((rows, 3072), og.dtype)] * 4
        + [pltpu.SemaphoreType.DMA((2, PEERS)), pltpu.SemaphoreType.DMA((4, PEERS // 2))],
        name="unpack",
    )(og, kv)


def nt(a, b):
    return lax.dot_general(a, b, (((1,), (1,)), ((), ())), preferred_element_type=jnp.float32)


def turned(row, size):
    return jnp.broadcast_to(row, (size, size)).T


def plan(pat_ref, tab_ref, ask_ref, base, z, x, heads, blocks, per_list):
    i32 = jnp.int32
    entries = blocks * per_list

    def grid(rows, columns, dim):
        return lax.broadcasted_iota(i32, (rows, columns), dim)

    def total(picked, value):
        return jnp.sum(jnp.where(picked, value, 0), axis=0, keepdims=True)

    def place(block):
        source = block >> 1
        rel = ((((source >> 2) - z) & 3) << 2) + (((source & 3) - x) & 3)
        return (((rel * STEP) & (PEERS - 1)) << 1) + (block & 1)

    def turn(ids):
        return jnp.where(ids < blocks, ids + 2 * CROSS, ids - blocks)

    rows = []
    hits = [jnp.zeros((1, 128), i32), jnp.zeros((1, 128), i32)]
    spot = grid(entries, 128, 1)
    for h in range(heads):
        pattern = pat_ref[h]
        mine = grid(per_list, entries, 1) // blocks == grid(per_list, entries, 0)
        rows.append(total(mine, jnp.concatenate([pattern] * per_list, axis=1)) - base)
        column = turned(rows[h], entries)[:, :128]
        for side, shift in enumerate((-blocks, blocks)):
            found = (column == spot + shift) & (spot < blocks)
            hits[side] = jnp.maximum(hits[side], jnp.max(found.astype(i32), axis=0, keepdims=True))
    down, across = grid(128, 128, 0), grid(128, 128, 1)
    ranks = []
    for side in range(2):
        hit = turned(hits[side], 128)
        rank = turned(total(down <= across, hit), 128)
        ranks.append(rank)
        ask_ref[side, 0:1] = total((hit > 0) & (rank == across + 1), place(down))
        back = jnp.where(hit > 0, rank - 1 + CROSS * side, 2 * CROSS)
        ask_ref[side, 1:2] = total((place(down) == across) & (down < blocks), back)
    number = grid(1, entries, 1)
    order = grid(entries, entries, 1)
    for h in range(heads):
        row = rows[h]
        block = grid(128, entries, 0)
        column = [jnp.concatenate([rank, rank], axis=1) for rank in ranks]
        outside = [total(block == row + shift, column[side] - 1) for side, shift in enumerate((blocks, -blocks))]
        ids = jnp.where(
            row < 0, blocks + outside[0], jnp.where(row < blocks, place(row), blocks + CROSS + outside[1])
        )
        key = turn(ids) * entries + number
        rank = total(turned(key, entries) < key, 1)
        column, rank = turned(ids, entries), turned(rank, entries)
        lands = rank == order
        ranked = total(lands, column)
        ahead = total(rank + 1 == order, column)
        tab_ref[h, 0:1] = ids
        tab_ref[h, 1:2] = total(lands, grid(entries, entries, 0))
        tab_ref[h, 2:3] = jnp.where((ranked == ahead) & (number > 0), 1, 0)
        upto = total(turn(column) <= turn(order), 1)
        held = total(column == order, 1)
        tab_ref[h, 3:4] = jnp.where(held > 0, upto - 1, entries)


def fused_kernel(
    pat_src, q_src, k_src, v_src, g_src, og_out, dkv_out,
    pat_ref, raw_q, raw_k, raw_v, raw_g, tabv, tab, askv, gotv, got,
    kvin, qgin, kvx, stage, kvw, kvt, terms, seg, ogs, dks, sums, back, near, sd0, sd1, ex0, ex1,
    in_send, in_recv, in_self, x_send, x_recv, b_send, b_recv, o_send, o_recv, o_self,
    raw_sem, pat_sem, tab_sem, got_sem, a_send, a_recv, q_recv,
    *, heads, blocks, per_list,
):
    bf16, f32 = jnp.bfloat16, jnp.float32
    me, slab = lax.axis_index("seq"), lax.axis_index("slab")
    slabs = lax.axis_size("slab")
    z, x = me // 4, me % 4
    entries = blocks * per_list
    after = {"slab": (slab + 1) % slabs}
    before = {"slab": (slab + slabs - 1) % slabs}

    def peer(dz, dx):
        return (z + dz) % 4 * 4 + (x + dx) % 4

    def remote(src, dst, send, recv, device):
        return pltpu.make_async_remote_copy(
            src_ref=src, dst_ref=dst, send_sem=send, recv_sem=recv, device_id=device, device_id_type=MESH
        )

    raws = ((k_src, raw_k), (v_src, raw_v), (q_src, raw_q), (g_src, raw_g))
    loads = [pltpu.make_async_copy(src, dst, raw_sem.at[i]) for i, (src, dst) in enumerate(raws)]
    for load in loads:
        load.start()
    pattern = pltpu.make_async_copy(pat_src, pat_ref, pat_sem.at[0])
    pattern.start()
    barrier = pltpu.get_barrier_semaphore()
    for dz, dx in SPREAD:
        pl.semaphore_signal(barrier, 1, device_id={"seq": peer(dz, dx)}, device_id_type=MESH)
    for device in (after, before):
        pl.semaphore_signal(barrier, 1, device_id=device, device_id_type=MESH)
    pl.semaphore_wait(barrier, len(SPREAD) + 2)

    inputs = ((raw_k, raw_v, ogs, kvin), (raw_q, raw_g, dks, qgin))

    def input_self(t, h):
        return pltpu.make_async_copy(
            inputs[t][2].at[h, pl.ds(0, 2)], inputs[t][3].at[h, pl.ds(0, 2)], in_self.at[t, h]
        )

    def send_input(t, h, p):
        rel = p * STEP % PEERS
        dz, dx = rel // 4, rel % 4
        slot = slot_of(4 - dz, 4 - dx)
        there = inputs[t][3].at[h, pl.ds(2 * slot, 2)]
        src = inputs[t][2].at[h, pl.ds(2 * p, 2)]
        landing = in_recv.at[h] if t == 0 else q_recv.at[h, slot]
        remote(src, there, in_send.at[t, h], landing, {"seq": peer(dz, dx)}).start()

    for h in range(heads):
        for t in range(2):
            if h == 0:
                loads[2 * t].wait()
                loads[2 * t + 1].wait()
            one, two, packed, _ = inputs[t]

            @pl.loop(0, PEERS)
            def _(p):
                rel = p * STEP % PEERS
                column = 3 * peer(rel // 4, rel % 4) + h
                lanes = pl.ds(pl.multiple_of(column // 2 * 128, 128), 128)

                for side in range(2):

                    @pl.when(column % 2 == side)
                    def _():
                        half = slice(HDIM * side, HDIM * side + HDIM)
                        for part in range(2):
                            rows = pl.ds(BLOCK * part, BLOCK)
                            a, b = one[rows, lanes], two[rows, lanes]
                            if t == 1:
                                a = a * jnp.asarray(SCALE, bf16)
                            packed[h, 2 * p + part] = jnp.concatenate([a[:, half], b[:, half]], axis=1)

                @pl.when(p == 1)
                def _():
                    input_self(t, h).start()

                @pl.when(p > 1)
                def _():
                    send_input(t, h, p - 1)

            send_input(t, h, PEERS - 1)

    def arrived(h):
        input_self(0, h).wait()
        rest = kvin.at[h, pl.ds(2, blocks - 2)]
        pltpu.make_async_copy(rest, rest, in_recv.at[h]).wait()

    def sent(t, h):
        rest = inputs[t][2].at[h, pl.ds(2, blocks - 2)]
        pltpu.make_async_copy(rest, rest, in_send.at[t, h]).wait()

    pattern.wait()
    plan(pat_ref, tabv, askv, slab * blocks, z, x, heads, blocks, per_list)
    asking = [remote(askv.at[i], gotv.at[i], a_send.at[i], a_recv.at[i], (before, after)[i]) for i in range(2)]
    for ask in asking:
        ask.start()
    table = pltpu.make_async_copy(tabv, tab, tab_sem.at[0])
    table.start()
    for ask in asking:
        ask.wait()
    gotten = pltpu.make_async_copy(gotv, got, got_sem.at[0])
    gotten.start()
    table.wait()
    gotten.wait()

    def crossing(h, side):
        return remote(
            stage.at[h, pl.ds(CROSS * side, CROSS)], kvx.at[h, pl.ds(CROSS * side, CROSS)],
            x_send.at[h, side], x_recv.at[h, side], (after, before)[side],
        )

    def returning(h, side):
        return remote(
            sums.at[h, pl.ds(CROSS * side, CROSS)], back.at[h, pl.ds(CROSS * side, CROSS)],
            b_send.at[h, side], b_recv.at[h, side], (before, after)[side],
        )

    def open_window(h):
        arrived(h)

        @pl.loop(0, blocks)
        def _(w):
            kvw[w] = kvin[h, w]

        for c in range(2 * CROSS):
            stage[h, c] = kvw[got[c // CROSS, 0, c % CROSS]]

        @pl.loop(0, blocks)
        def _(w):
            kvt[w] = kvin[h, w].T

        for side in range(2):
            crossing(h, side).start()

    seg[entries] = jnp.zeros((BLOCK, 128), bf16)
    near[2 * CROSS] = jnp.zeros((BLOCK, 128), bf16)
    left = lax.broadcasted_iota(jnp.int32, (BLOCK, 128), 1) < HDIM
    open_window(0)

    def output(src, dst, t, h, p):
        rel = p * STEP % PEERS
        dz, dx = rel // 4, rel % 4
        there = slot_of(4 - dz, 4 - dx)
        return remote(src.at[h, pl.ds(2 * p, 2)], dst.at[h, there], o_send.at[t, h], o_recv.at[t, h], {"seq": peer(dz, dx)})

    def output_self(src, dst, t, h):
        return pltpu.make_async_copy(src.at[h, pl.ds(0, 2)], dst.at[h, 0], o_self.at[t, h])

    @pl.loop(0, heads)
    def _(h):
        for side in range(2):
            crossing(h, side).wait_recv()
        for c in range(2 * CROSS):
            block = kvx[h, c]
            kvw[blocks + c] = block
            kvt[blocks + c] = block.T
        sent(0, h)

        @pl.loop(0, blocks // 2)
        def _(p):
            @pl.when(p == 0)
            def _():
                input_self(1, h).wait()

            @pl.when(p > 0)
            def _():
                chunk = qgin.at[h, pl.ds(2 * p, 2)]
                pltpu.make_async_copy(chunk, chunk, q_recv.at[h, p]).wait()

            @pl.when(p == 1)
            def _():
                output_self(ogs, og_out, 0, h).start()

            @pl.when(p > 1)
            def _():
                output(ogs, og_out, 0, h, p - 1).start()

            rel = p * STEP % PEERS
            first = 2 * peer(rel // 4, rel % 4)
            pairs = []
            for half, (sd, ex) in enumerate(((sd0, ex0), (sd1, ex1))):
                b = 2 * p + half
                qg = qgin[h, b]
                zero = jnp.zeros_like(qg)
                both = jnp.concatenate([jnp.where(left, qg, zero), jnp.where(left, zero, qg)], axis=0)
                base = first + half
                ids = [tab[h, 0, base + j * blocks] for j in range(per_list)]
                top = None
                for j in range(per_list):
                    pair = nt(kvw[ids[j]], both)
                    sd[j] = pair
                    part = jnp.max(pair[:, :BLOCK].reshape(16, 8, BLOCK), axis=0)
                    top = part if top is None else jnp.maximum(top, part)
                pairs.append((b, base, sd, ex, both, ids, jnp.max(top, axis=0, keepdims=True)))
            for b, base, sd, ex, both, ids, row_max in pairs:
                total = jnp.zeros((8, BLOCK), f32)
                mixed = jnp.zeros((8, BLOCK), f32)
                for j in range(per_list):
                    e = jnp.exp(sd[j, :, :BLOCK] - row_max)
                    sd[j, :, :BLOCK] = e
                    ex[j, :, BLOCK:] = e.astype(bf16)
                    total += jnp.sum(e.reshape(16, 8, BLOCK), axis=0)
                    mixed += jnp.sum((e * sd[j, :, BLOCK:]).reshape(16, 8, BLOCK), axis=0)
                inverse = 1.0 / jnp.sum(total, axis=0, keepdims=True)
                correction = jnp.sum(mixed, axis=0, keepdims=True) * inverse
                for j in range(per_list):
                    ex[j, :, :BLOCK] = (sd[j, :, :BLOCK] * (sd[j, :, BLOCK:] - correction)).astype(bf16)
                out = jnp.zeros((128, 2 * BLOCK), f32)
                for j in range(0, per_list, 2):
                    lhs = jnp.concatenate([kvt[ids[j]], kvt[ids[j + 1]]], axis=1)
                    rhs = ex[j : j + 2].reshape(2 * BLOCK, 2 * BLOCK)
                    out += jnp.dot(lhs, rhs, preferred_element_type=f32)
                outs = jnp.concatenate([out[:HDIM, :BLOCK] * (inverse * SCALE), out[HDIM:, BLOCK:] * inverse], axis=0)
                ogs[h, b] = outs.T.astype(bf16)
                column = jnp.broadcast_to(inverse, (BLOCK, BLOCK)).T
                scaled = (both.astype(f32) * jnp.concatenate([column, column], axis=0)).astype(bf16)
                for j in range(per_list):
                    terms[base + j * blocks] = jnp.dot(ex[j], scaled, preferred_element_type=f32)

        @pl.when(h + 1 < heads)
        def _():
            open_window(h + 1)

        output(ogs, og_out, 0, h, blocks // 2 - 1).start()

        def running(t, acc):
            keep = tab[h, 2, t].astype(f32)
            acc = acc * keep + terms[tab[h, 1, t]]
            seg[t] = acc.astype(bf16)
            return acc

        acc = lax.fori_loop(0, entries // 2, running, jnp.zeros((BLOCK, 128), f32))
        for c in range(2 * CROSS):
            sums[h, c] = seg[tab[h, 3, blocks + c]]
        acc = lax.fori_loop(entries // 2, entries // 2 + 8, running, acc)
        for side in range(2):
            returning(h, side).start()
        lax.fori_loop(entries // 2 + 8, entries, running, acc)
        sent(1, h)
        for side in range(2):
            returning(h, side).wait_recv()
        for c in range(2 * CROSS):
            near[c] = back[h, c]

        @pl.loop(0, blocks // 2)
        def _(p):
            for half in range(2):
                w = 2 * p + half
                total = seg[tab[h, 3, w]].astype(f32)
                total += near[got[0, 1, w]].astype(f32)
                total += near[got[1, 1, w]].astype(f32)
                dks[h, w] = total.astype(bf16)

            @pl.when(p == 1)
            def _():
                output_self(dks, dkv_out, 1, h).start()

            @pl.when(p > 1)
            def _():
                output(dks, dkv_out, 1, h, p - 1).start()

        output(dks, dkv_out, 1, h, blocks // 2 - 1).start()

    for h in range(heads):
        for side in range(2):
            crossing(h, side).wait_send()
            returning(h, side).wait_send()
        for t, (src, dst) in enumerate(((ogs, og_out), (dks, dkv_out))):
            output_self(src, dst, t, h).wait()
            rest = src.at[h, pl.ds(2, blocks - 2)]
            pltpu.make_async_copy(rest, rest, o_send.at[t, h]).wait()
            landed = dst.at[h, pl.ds(1, PEERS - 1)]
            pltpu.make_async_copy(landed, landed, o_recv.at[t, h]).wait()


def fused(pattern, q, k, v, g):
    heads, per_list, blocks = pattern.shape
    f32, bf16 = jnp.float32, jnp.bfloat16
    window = blocks + 2 * CROSS
    entries = blocks * per_list
    block = (BLOCK, 128)
    sems = pltpu.SemaphoreType.DMA
    out = jax.ShapeDtypeStruct((heads, PEERS, 2, BLOCK, 128), bf16)
    any_spec = pl.BlockSpec(memory_space=pl.ANY)
    return pl.pallas_call(
        functools.partial(fused_kernel, heads=heads, blocks=blocks, per_list=per_list),
        in_specs=[any_spec] * 5,
        out_specs=[any_spec, any_spec],
        out_shape=[out, out],
        scratch_shapes=[pltpu.VMEM(pattern.shape, jnp.int32)]
        + [pltpu.VMEM(q.shape, bf16)] * 4
        + [
            pltpu.VMEM((heads, 8, entries), jnp.int32),
            pltpu.SMEM((heads, 8, entries), jnp.int32),
            pltpu.VMEM((2, 8, 128), jnp.int32),
            pltpu.VMEM((2, 8, 128), jnp.int32),
            pltpu.SMEM((2, 8, 128), jnp.int32),
            pltpu.VMEM((heads, blocks, *block), bf16),
            pltpu.VMEM((heads, blocks, *block), bf16),
            pltpu.VMEM((heads, 2 * CROSS, *block), bf16),
            pltpu.VMEM((heads, 2 * CROSS, *block), bf16),
            pltpu.VMEM((window, *block), bf16),
            pltpu.VMEM((window, *block), bf16),
            pltpu.VMEM((entries, *block), f32),
            pltpu.VMEM((entries + 1, *block), bf16),
            pltpu.VMEM((heads, blocks, *block), bf16),
            pltpu.VMEM((heads, blocks, *block), bf16),
            pltpu.VMEM((heads, 2 * CROSS, *block), bf16),
            pltpu.VMEM((heads, 2 * CROSS, *block), bf16),
            pltpu.VMEM((2 * CROSS + 1, *block), bf16),
            pltpu.VMEM((per_list, BLOCK, 2 * BLOCK), f32),
            pltpu.VMEM((per_list, BLOCK, 2 * BLOCK), f32),
            pltpu.VMEM((per_list, BLOCK, 2 * BLOCK), bf16),
            pltpu.VMEM((per_list, BLOCK, 2 * BLOCK), bf16),
        ]
        + [sems((2, heads)), sems((heads,)), sems((2, heads))]
        + [sems((heads, 2))] * 4
        + [sems((2, heads))] * 3
        + [sems((4,)), sems((1,)), sems((1,)), sems((1,)), sems((2,)), sems((2,)), sems((heads, PEERS))],
        compiler_params=pltpu.CompilerParams(
            collective_id=0, has_side_effects=True, vmem_limit_bytes=60 << 20
        ),
        name="fused",
    )(pattern, q, k, v, g)


def local(query, key, value, d_out, pattern):
    og, dkv = fused(jnp.transpose(pattern, (0, 2, 1)), query, key, value, d_out)
    return tuple(unpack(og, dkv))


def solution(mesh):
    rows = P(("slab", "seq"), None)
    return jax.shard_map(
        local,
        mesh=mesh,
        in_specs=(rows, rows, rows, rows, P("seq", "slab", None)),
        out_specs=(rows, rows, rows, rows),
        check_vma=False,
    )
```

```python
import functools

import jax
import jax.numpy as jnp
from jax import lax
from jax.experimental import pallas as pl
from jax.experimental.pallas import tpu as pltpu
from jax.sharding import PartitionSpec as P

CROSS = 4
HDIM = 64
BLOCK = 128
SCALE = HDIM**-0.5
PEERS = 16
STEP = 7
MESH = pl.DeviceIdType.MESH
SPREAD = ((0, 1), (1, 0), (0, 3), (3, 0), (1, 1), (3, 3), (1, 3), (3, 1), (0, 2), (2, 0), (1, 2), (2, 1), (3, 2), (2, 3), (2, 2))


def slot_of(dz, dx):
    return ((dz % 4) * 4 + dx % 4) * STEP % PEERS


def unpack_kernel(og_src, kv_src, o_out, dq_out, dk_out, dv_out, og, kv, o_ref, dq_ref, dk_ref, dv_ref, in_sem, out_sem):
    me = lax.axis_index("seq")
    z, x = me // 4, me % 4
    loads = []
    for g in range(PEERS):
        slot = slot_of(g // 4 - z + 4, g % 4 - x + 4)
        pair = [
            pltpu.make_async_copy(src.at[:, slot], dst.at[g], in_sem.at[i, g])
            for i, (src, dst) in enumerate(((og_src, og), (kv_src, kv)))
        ]
        for load in pair:
            load.start()
        loads.append(pair)
    left = lax.broadcasted_iota(jnp.int32, (BLOCK, 128), 1) < HDIM
    stores = []
    for i in range(PEERS // 2):
        for g in (2 * i, 2 * i + 1):
            for load in loads[g]:
                load.wait()
        for t in range(3):
            cols = slice(384 * i + 128 * t, 384 * i + 128 * t + 128)
            a, b = 6 * i + 2 * t, 6 * i + 2 * t + 1
            for part in range(2):
                rows = slice(BLOCK * part, BLOCK * part + BLOCK)
                for src, low, high in ((og, dq_ref, o_ref), (kv, dk_ref, dv_ref)):
                    one, two = src[a // 3, a % 3, part], src[b // 3, b % 3, part]
                    low[rows, cols] = jnp.where(left, one, pltpu.roll(two, HDIM, 1))
                    high[rows, cols] = jnp.where(left, pltpu.roll(one, HDIM, 1), two)
        cols = slice(384 * i, 384 * i + 384)
        for n, (src, dst) in enumerate(((o_ref, o_out), (dq_ref, dq_out), (dk_ref, dk_out), (dv_ref, dv_out))):
            store = pltpu.make_async_copy(src.at[:, cols], dst.at[:, cols], out_sem.at[n, i])
            store.start()
            stores.append(store)
    for store in stores:
        store.wait()


def unpack(og, kv):
    rows = 2 * BLOCK
    any_spec = pl.BlockSpec(memory_space=pl.ANY)
    out = jax.ShapeDtypeStruct((rows, 3072), og.dtype)
    return pl.pallas_call(
        unpack_kernel,
        in_specs=[any_spec] * 2,
        out_specs=[any_spec] * 4,
        out_shape=[out] * 4,
        scratch_shapes=[pltpu.VMEM((PEERS, 3, 2, BLOCK, 128), og.dtype)] * 2
        + [pltpu.VMEM((rows, 3072), og.dtype)] * 4
        + [pltpu.SemaphoreType.DMA((2, PEERS)), pltpu.SemaphoreType.DMA((4, PEERS // 2))],
        name="unpack",
    )(og, kv)


def nt(a, b):
    return lax.dot_general(a, b, (((1,), (1,)), ((), ())), preferred_element_type=jnp.float32)


def turned(row, size):
    return jnp.broadcast_to(row, (size, size)).T


def plan(pat_ref, tab_ref, ask_ref, base, z, x, heads, blocks, per_list):
    i32 = jnp.int32
    entries = blocks * per_list

    def grid(rows, columns, dim):
        return lax.broadcasted_iota(i32, (rows, columns), dim)

    def total(picked, value):
        return jnp.sum(jnp.where(picked, value, 0), axis=0, keepdims=True)

    def place(block):
        source = block >> 1
        rel = ((((source >> 2) - z) & 3) << 2) + (((source & 3) - x) & 3)
        return (((rel * STEP) & (PEERS - 1)) << 1) + (block & 1)

    def turn(ids):
        return jnp.where(ids < blocks, ids + 2 * CROSS, ids - blocks)

    rows = []
    hits = [jnp.zeros((1, 128), i32), jnp.zeros((1, 128), i32)]
    spot = grid(entries, 128, 1)
    for h in range(heads):
        pattern = pat_ref[h]
        mine = grid(per_list, entries, 1) // blocks == grid(per_list, entries, 0)
        rows.append(total(mine, jnp.concatenate([pattern] * per_list, axis=1)) - base)
        column = turned(rows[h], entries)[:, :128]
        for side, shift in enumerate((-blocks, blocks)):
            found = (column == spot + shift) & (spot < blocks)
            hits[side] = jnp.maximum(hits[side], jnp.max(found.astype(i32), axis=0, keepdims=True))
    down, across = grid(128, 128, 0), grid(128, 128, 1)
    ranks = []
    for side in range(2):
        hit = turned(hits[side], 128)
        rank = turned(total(down <= across, hit), 128)
        ranks.append(rank)
        ask_ref[side, 0:1] = total((hit > 0) & (rank == across + 1), place(down))
        back = jnp.where(hit > 0, rank - 1 + CROSS * side, 2 * CROSS)
        ask_ref[side, 1:2] = total((place(down) == across) & (down < blocks), back)
    number = grid(1, entries, 1)
    order = grid(entries, entries, 1)
    for h in range(heads):
        row = rows[h]
        block = grid(128, entries, 0)
        column = [jnp.concatenate([rank, rank], axis=1) for rank in ranks]
        outside = [total(block == row + shift, column[side] - 1) for side, shift in enumerate((blocks, -blocks))]
        ids = jnp.where(
            row < 0, blocks + outside[0], jnp.where(row < blocks, place(row), blocks + CROSS + outside[1])
        )
        key = turn(ids) * entries + number
        rank = total(turned(key, entries) < key, 1)
        column, rank = turned(ids, entries), turned(rank, entries)
        lands = rank == order
        ranked = total(lands, column)
        ahead = total(rank + 1 == order, column)
        tab_ref[h, 0:1] = ids
        tab_ref[h, 1:2] = total(lands, grid(entries, entries, 0))
        tab_ref[h, 2:3] = jnp.where((ranked == ahead) & (number > 0), 1, 0)
        upto = total(turn(column) <= turn(order), 1)
        held = total(column == order, 1)
        tab_ref[h, 3:4] = jnp.where(held > 0, upto - 1, entries)


def fused_kernel(
    pat_src, q_src, k_src, v_src, g_src, og_out, dkv_out,
    pat_ref, raw_q, raw_k, raw_v, raw_g, tabv, tab, askv, gotv, got,
    kvin, qgin, kvx, stage, kvw, kvt, terms, seg, ogs, dks, sums, back, near, sd0, sd1, ex0, ex1,
    in_send, in_recv, in_self, x_send, x_recv, b_send, b_recv, o_send, o_recv, o_self,
    raw_sem, pat_sem, tab_sem, got_sem, a_send, a_recv, q_recv,
    *, heads, blocks, per_list,
):
    bf16, f32 = jnp.bfloat16, jnp.float32
    me, slab = lax.axis_index("seq"), lax.axis_index("slab")
    slabs = lax.axis_size("slab")
    z, x = me // 4, me % 4
    entries = blocks * per_list
    after = {"slab": (slab + 1) % slabs}
    before = {"slab": (slab + slabs - 1) % slabs}

    def peer(dz, dx):
        return (z + dz) % 4 * 4 + (x + dx) % 4

    def remote(src, dst, send, recv, device):
        return pltpu.make_async_remote_copy(
            src_ref=src, dst_ref=dst, send_sem=send, recv_sem=recv, device_id=device, device_id_type=MESH
        )

    raws = ((k_src, raw_k), (v_src, raw_v), (q_src, raw_q), (g_src, raw_g))
    loads = [pltpu.make_async_copy(src, dst, raw_sem.at[i]) for i, (src, dst) in enumerate(raws)]
    for load in loads:
        load.start()
    pattern = pltpu.make_async_copy(pat_src, pat_ref, pat_sem.at[0])
    pattern.start()
    barrier = pltpu.get_barrier_semaphore()
    for dz, dx in SPREAD:
        pl.semaphore_signal(barrier, 1, device_id={"seq": peer(dz, dx)}, device_id_type=MESH)
    for device in (after, before):
        pl.semaphore_signal(barrier, 1, device_id=device, device_id_type=MESH)
    pl.semaphore_wait(barrier, len(SPREAD) + 2)

    inputs = ((raw_k, raw_v, ogs, kvin), (raw_q, raw_g, dks, qgin))

    def input_self(t, h):
        return pltpu.make_async_copy(
            inputs[t][2].at[h, pl.ds(0, 2)], inputs[t][3].at[h, pl.ds(0, 2)], in_self.at[t, h]
        )

    def send_input(t, h, p):
        rel = p * STEP % PEERS
        dz, dx = rel // 4, rel % 4
        slot = slot_of(4 - dz, 4 - dx)
        there = inputs[t][3].at[h, pl.ds(2 * slot, 2)]
        src = inputs[t][2].at[h, pl.ds(2 * p, 2)]
        landing = in_recv.at[h] if t == 0 else q_recv.at[h, slot]
        remote(src, there, in_send.at[t, h], landing, {"seq": peer(dz, dx)}).start()

    for h in range(heads):
        for t in range(2):
            if h == 0:
                loads[2 * t].wait()
                loads[2 * t + 1].wait()
            one, two, packed, _ = inputs[t]

            @pl.loop(0, PEERS)
            def _(p):
                rel = p * STEP % PEERS
                column = 3 * peer(rel // 4, rel % 4) + h
                lanes = pl.ds(pl.multiple_of(column // 2 * 128, 128), 128)

                for side in range(2):

                    @pl.when(column % 2 == side)
                    def _():
                        half = slice(HDIM * side, HDIM * side + HDIM)
                        for part in range(2):
                            rows = pl.ds(BLOCK * part, BLOCK)
                            a, b = one[rows, lanes], two[rows, lanes]
                            if t == 1:
                                a = a * jnp.asarray(SCALE, bf16)
                            packed[h, 2 * p + part] = jnp.concatenate([a[:, half], b[:, half]], axis=1)

                @pl.when(p == 1)
                def _():
                    input_self(t, h).start()

                @pl.when(p > 1)
                def _():
                    send_input(t, h, p - 1)

            send_input(t, h, PEERS - 1)

    def arrived(h):
        input_self(0, h).wait()
        rest = kvin.at[h, pl.ds(2, blocks - 2)]
        pltpu.make_async_copy(rest, rest, in_recv.at[h]).wait()

    def sent(t, h):
        rest = inputs[t][2].at[h, pl.ds(2, blocks - 2)]
        pltpu.make_async_copy(rest, rest, in_send.at[t, h]).wait()

    pattern.wait()
    plan(pat_ref, tabv, askv, slab * blocks, z, x, heads, blocks, per_list)
    asking = [remote(askv.at[i], gotv.at[i], a_send.at[i], a_recv.at[i], (before, after)[i]) for i in range(2)]
    for ask in asking:
        ask.start()
    table = pltpu.make_async_copy(tabv, tab, tab_sem.at[0])
    table.start()
    for ask in asking:
        ask.wait()
    gotten = pltpu.make_async_copy(gotv, got, got_sem.at[0])
    gotten.start()
    table.wait()
    gotten.wait()

    def crossing(h, side):
        return remote(
            stage.at[h, pl.ds(CROSS * side, CROSS)], kvx.at[h, pl.ds(CROSS * side, CROSS)],
            x_send.at[h, side], x_recv.at[h, side], (after, before)[side],
        )

    def returning(h, side):
        return remote(
            sums.at[h, pl.ds(CROSS * side, CROSS)], back.at[h, pl.ds(CROSS * side, CROSS)],
            b_send.at[h, side], b_recv.at[h, side], (before, after)[side],
        )

    def open_window(h):
        arrived(h)

        @pl.loop(0, blocks)
        def _(w):
            kvw[w] = kvin[h, w]

        for c in range(2 * CROSS):
            stage[h, c] = kvw[got[c // CROSS, 0, c % CROSS]]

        @pl.loop(0, blocks)
        def _(w):
            kvt[w] = kvin[h, w].T

        for side in range(2):
            crossing(h, side).start()

    seg[entries] = jnp.zeros((BLOCK, 128), bf16)
    near[2 * CROSS] = jnp.zeros((BLOCK, 128), bf16)
    left = lax.broadcasted_iota(jnp.int32, (BLOCK, 128), 1) < HDIM
    open_window(0)

    def output(src, dst, t, h, p):
        rel = p * STEP % PEERS
        dz, dx = rel // 4, rel % 4
        there = slot_of(4 - dz, 4 - dx)
        return remote(src.at[h, pl.ds(2 * p, 2)], dst.at[h, there], o_send.at[t, h], o_recv.at[t, h], {"seq": peer(dz, dx)})

    def output_self(src, dst, t, h):
        return pltpu.make_async_copy(src.at[h, pl.ds(0, 2)], dst.at[h, 0], o_self.at[t, h])

    @pl.loop(0, heads)
    def _(h):
        for side in range(2):
            crossing(h, side).wait_recv()
        for c in range(2 * CROSS):
            block = kvx[h, c]
            kvw[blocks + c] = block
            kvt[blocks + c] = block.T
        sent(0, h)

        @pl.loop(0, blocks // 2)
        def _(p):
            @pl.when(p == 0)
            def _():
                input_self(1, h).wait()

            @pl.when(p > 0)
            def _():
                chunk = qgin.at[h, pl.ds(2 * p, 2)]
                pltpu.make_async_copy(chunk, chunk, q_recv.at[h, p]).wait()

            @pl.when(p == 1)
            def _():
                output_self(ogs, og_out, 0, h).start()

            @pl.when(p > 1)
            def _():
                output(ogs, og_out, 0, h, p - 1).start()

            rel = p * STEP % PEERS
            first = 2 * peer(rel // 4, rel % 4)
            pairs = []
            for half, (sd, ex) in enumerate(((sd0, ex0), (sd1, ex1))):
                b = 2 * p + half
                qg = qgin[h, b]
                zero = jnp.zeros_like(qg)
                both = jnp.concatenate([jnp.where(left, qg, zero), jnp.where(left, zero, qg)], axis=0)
                base = first + half
                ids = [tab[h, 0, base + j * blocks] for j in range(per_list)]
                top = None
                for j in range(per_list):
                    pair = nt(kvw[ids[j]], both)
                    sd[j] = pair
                    part = jnp.max(pair[:, :BLOCK].reshape(16, 8, BLOCK), axis=0)
                    top = part if top is None else jnp.maximum(top, part)
                pairs.append((b, base, sd, ex, both, ids, jnp.max(top, axis=0, keepdims=True)))
            for b, base, sd, ex, both, ids, row_max in pairs:
                total = jnp.zeros((8, BLOCK), f32)
                mixed = jnp.zeros((8, BLOCK), f32)
                for j in range(per_list):
                    e = jnp.exp(sd[j, :, :BLOCK] - row_max)
                    sd[j, :, :BLOCK] = e
                    total += jnp.sum(e.reshape(16, 8, BLOCK), axis=0)
                    mixed += jnp.sum((e * sd[j, :, BLOCK:]).reshape(16, 8, BLOCK), axis=0)
                inverse = 1.0 / jnp.sum(total, axis=0, keepdims=True)
                correction = jnp.sum(mixed, axis=0, keepdims=True) * inverse
                for j in range(per_list):
                    weights = sd[j, :, :BLOCK] * inverse
                    ex[j, :, BLOCK:] = weights.astype(bf16)
                    ex[j, :, :BLOCK] = (weights * (sd[j, :, BLOCK:] - correction)).astype(bf16)
                out = jnp.zeros((128, 2 * BLOCK), f32)
                for j in range(0, per_list, 2):
                    lhs = jnp.concatenate([kvt[ids[j]], kvt[ids[j + 1]]], axis=1)
                    rhs = ex[j : j + 2].reshape(2 * BLOCK, 2 * BLOCK)
                    out += jnp.dot(lhs, rhs, preferred_element_type=f32)
                outs = jnp.concatenate([out[:HDIM, :BLOCK] * SCALE, out[HDIM:, BLOCK:]], axis=0)
                ogs[h, b] = outs.T.astype(bf16)
                for j in range(per_list):
                    terms[base + j * blocks] = jnp.dot(ex[j], both, preferred_element_type=f32)

        @pl.when(h + 1 < heads)
        def _():
            open_window(h + 1)

        output(ogs, og_out, 0, h, blocks // 2 - 1).start()

        def running(t, acc):
            keep = tab[h, 2, t].astype(f32)
            acc = acc * keep + terms[tab[h, 1, t]]
            seg[t] = acc.astype(bf16)
            return acc

        acc = lax.fori_loop(0, entries // 2, running, jnp.zeros((BLOCK, 128), f32))
        for c in range(2 * CROSS):
            sums[h, c] = seg[tab[h, 3, blocks + c]]
        acc = lax.fori_loop(entries // 2, entries // 2 + 8, running, acc)
        for side in range(2):
            returning(h, side).start()
        lax.fori_loop(entries // 2 + 8, entries, running, acc)
        sent(1, h)
        for side in range(2):
            returning(h, side).wait_recv()
        for c in range(2 * CROSS):
            near[c] = back[h, c]

        @pl.loop(0, blocks // 2)
        def _(p):
            for half in range(2):
                w = 2 * p + half
                total = seg[tab[h, 3, w]].astype(f32)
                total += near[got[0, 1, w]].astype(f32)
                total += near[got[1, 1, w]].astype(f32)
                dks[h, w] = total.astype(bf16)

            @pl.when(p == 1)
            def _():
                output_self(dks, dkv_out, 1, h).start()

            @pl.when(p > 1)
            def _():
                output(dks, dkv_out, 1, h, p - 1).start()

        output(dks, dkv_out, 1, h, blocks // 2 - 1).start()

    for h in range(heads):
        for side in range(2):
            crossing(h, side).wait_send()
            returning(h, side).wait_send()
        for t, (src, dst) in enumerate(((ogs, og_out), (dks, dkv_out))):
            output_self(src, dst, t, h).wait()
            rest = src.at[h, pl.ds(2, blocks - 2)]
            pltpu.make_async_copy(rest, rest, o_send.at[t, h]).wait()
            landed = dst.at[h, pl.ds(1, PEERS - 1)]
            pltpu.make_async_copy(landed, landed, o_recv.at[t, h]).wait()


def fused(pattern, q, k, v, g):
    heads, per_list, blocks = pattern.shape
    f32, bf16 = jnp.float32, jnp.bfloat16
    window = blocks + 2 * CROSS
    entries = blocks * per_list
    block = (BLOCK, 128)
    sems = pltpu.SemaphoreType.DMA
    out = jax.ShapeDtypeStruct((heads, PEERS, 2, BLOCK, 128), bf16)
    any_spec = pl.BlockSpec(memory_space=pl.ANY)
    return pl.pallas_call(
        functools.partial(fused_kernel, heads=heads, blocks=blocks, per_list=per_list),
        in_specs=[any_spec] * 5,
        out_specs=[any_spec, any_spec],
        out_shape=[out, out],
        scratch_shapes=[pltpu.VMEM(pattern.shape, jnp.int32)]
        + [pltpu.VMEM(q.shape, bf16)] * 4
        + [
            pltpu.VMEM((heads, 8, entries), jnp.int32),
            pltpu.SMEM((heads, 8, entries), jnp.int32),
            pltpu.VMEM((2, 8, 128), jnp.int32),
            pltpu.VMEM((2, 8, 128), jnp.int32),
            pltpu.SMEM((2, 8, 128), jnp.int32),
            pltpu.VMEM((heads, blocks, *block), bf16),
            pltpu.VMEM((heads, blocks, *block), bf16),
            pltpu.VMEM((heads, 2 * CROSS, *block), bf16),
            pltpu.VMEM((heads, 2 * CROSS, *block), bf16),
            pltpu.VMEM((window, *block), bf16),
            pltpu.VMEM((window, *block), bf16),
            pltpu.VMEM((entries, *block), f32),
            pltpu.VMEM((entries + 1, *block), bf16),
            pltpu.VMEM((heads, blocks, *block), bf16),
            pltpu.VMEM((heads, blocks, *block), bf16),
            pltpu.VMEM((heads, 2 * CROSS, *block), bf16),
            pltpu.VMEM((heads, 2 * CROSS, *block), bf16),
            pltpu.VMEM((2 * CROSS + 1, *block), bf16),
            pltpu.VMEM((per_list, BLOCK, 2 * BLOCK), f32),
            pltpu.VMEM((per_list, BLOCK, 2 * BLOCK), f32),
            pltpu.VMEM((per_list, BLOCK, 2 * BLOCK), bf16),
            pltpu.VMEM((per_list, BLOCK, 2 * BLOCK), bf16),
        ]
        + [sems((2, heads)), sems((heads,)), sems((2, heads))]
        + [sems((heads, 2))] * 4
        + [sems((2, heads))] * 3
        + [sems((4,)), sems((1,)), sems((1,)), sems((1,)), sems((2,)), sems((2,)), sems((heads, PEERS))],
        compiler_params=pltpu.CompilerParams(
            collective_id=0, has_side_effects=True, vmem_limit_bytes=60 << 20
        ),
        name="fused",
    )(pattern, q, k, v, g)


def local(query, key, value, d_out, pattern):
    og, dkv = fused(jnp.transpose(pattern, (0, 2, 1)), query, key, value, d_out)
    return tuple(unpack(og, dkv))


def solution(mesh):
    rows = P(("slab", "seq"), None)
    return jax.shard_map(
        local,
        mesh=mesh,
        in_specs=(rows, rows, rows, rows, P("seq", "slab", None)),
        out_specs=(rows, rows, rows, rows),
        check_vma=False,
    )
```
